32 devices in a mesh: tile: 4 (over z), lat: 4 (over y, x), emu: 2 (over core).
Axes of the slice: x: 2, y: 2, z: 4, core: 2. Of those that a mesh axis runs over, the one named last changes fastest.
Arguments:
- state: float32 [64, 128, 12, 128], P('tile', ('lat', 'emu')), may hold values from -6 to 6
- diffusivity: float32 [12, 128], replicated, may hold values from 0.03 to 0.2
- wind: float32 [64, 128], P('tile', ('lat', 'emu')), may hold values from -0.5 to 0.5
- land_mask: int32 [64, 128], P('tile', ('lat', 'emu')), may hold values 0 or 1
- routes: int32 [4, 4, 2, 256, 1], P('tile', 'lat', 'emu'), may hold values from 0 to 15; in each aligned block of 256 rows (0 to 255, 256 to 511, ..., all dimensions but the last counted through in order) at most 20 rows name the same one
- counts: int32 [4, 4, 2], P('tile', 'lat', 'emu'), may hold values from 64 to 256
- w_in: bfloat16 [16, 1536, 1024], P(('tile', 'lat')), may hold values from -0.15625 to 0.15625
- b_in: float32 [16, 1024], P(('tile', 'lat')), may hold values from -3 to 3
- land_vec: float32 [16, 1024], P(('tile', 'lat')), may hold values from -5 to 5
- w_hid: bfloat16 [16, 2, 1024, 1024], P(('tile', 'lat')), may hold values from -0.1875 to 0.1875
- b_hid: float32 [16, 2, 1024], P(('tile', 'lat')), may hold values from -3 to 3
- w_out: bfloat16 [16, 1024, 512], P(('tile', 'lat')), may hold values from -0.1875 to 0.1875
Outputs:
- updated: float32 [64, 128, 4, 128], P('tile', ('lat', 'emu'))
The draws below stay inside these ranges and needn't reach their ends.
Inputs may be any that keep to these rules, and one draw needn't show every extreme that they name: `routes`: among the 256 columns of one device, at most 20 name the same expert.
All inputs are finite; a program needn't handle non-finite values. No bound on the sum of `land_mask` on one device may be relied on, other than what follows from the above.
Results may differ from the reference program's by a relative error of at most 0.0026.
Values may be sent and summed in bfloat16 or wider, within the bound.
No kernel may reach another device: no remote copies, remote signals or barrier semaphores. Data moves between devices by JAX's collectives and lax.ppermute only.
A program may use at most 64 MiB of HBM per device.

```python
import math
import jax
import jax.numpy as jnp
import numpy as np
from jax import lax

LEV = 128
VARS = 12
HID = 1024
OUTV = 4
LAYERS = 2
CLON = 16
CLAT = 16
COLS_DEV = 256
EXPERTS = 16
CAP = 20
NLON = 64
NLAT = 128
N_TILE = 4
N_LAT = 4
N_EMU = 2


def set_ends(values, own_key, smallest, largest):
    spot = [jax.random.randint(jax.random.fold_in(own_key, axis), (), 0, length) for axis, length in enumerate(values.shape)]
    longest = values.shape.index(max(values.shape))
    neighbour = spot[:longest] + [(spot[longest] + 1) % values.shape[longest]] + spot[longest + 1:]
    return values.at[tuple(spot)].set(smallest).at[tuple(neighbour)].set(largest)


def shard_levels(stream_key, dims, pieces, low, largest):
    def one(dim, blocks):
        steps = jax.random.uniform(jax.random.fold_in(jax.random.fold_in(stream_key, 6), dim), (blocks,), jnp.float32, low / len(pieces), largest / len(pieces))
        return jnp.repeat(jnp.exp(steps), dims[dim] // blocks).reshape((-1,) + (1,) * (len(dims) - dim - 1))

    level = one(*pieces[0])
    for cut in pieces[1:]:
        level = level * one(*cut)
    return level


def deal_out(rng, own, number, rows, amount, top, most, skew):
    order = jax.random.permutation(rng, amount)
    heavy_load, usual = portions_of(amount, rows * top, most, skew, True), portions_of(amount, rows * top, most, skew, False)
    places = jnp.arange(amount)

    def named(tallies, rotation):
        used = int((tallies > 0).sum())
        fixed = max(1, used // 4)
        moved = fixed + (places - fixed + rotation * (used - fixed)) % max(1, amount - fixed)
        return jnp.zeros((amount,), jnp.int32).at[order[jnp.where(places < fixed, places, moved)]].set(jnp.asarray(tallies, jnp.int32))

    tallies = jnp.where(number % 4 == 0, named(heavy_load, number // 4), named(usual, number - number // 4 - 1))
    mixed = jax.random.permutation(jax.random.fold_in(own, 3), amount)
    source_of, sink = mixed[0:amount // 2 * 2:2], mixed[1:amount // 2 * 2:2]
    room = jnp.minimum(tallies[source_of] - 1, most - tallies[sink]) // 2
    room = jnp.where((source_of == order[0]) | (sink == order[0]) | (tallies[sink] == 0), 0, jnp.maximum(room, 0))
    moved = jax.random.randint(jax.random.fold_in(own, 4), (amount // 2,), 0, 1 << 20) % (room + 1)
    tallies = tallies.at[source_of].add(-moved).at[sink].add(moved)
    members = jnp.searchsorted(jnp.cumsum(tallies), jnp.arange(rows * top), side="right").astype(jnp.int32)
    listing = members.reshape(top, rows).T
    listing = listing[jax.random.permutation(jax.random.fold_in(own, 1), rows)]
    rotation = jax.random.randint(jax.random.fold_in(own, 2), (rows, 1), 0, top)
    return jnp.take_along_axis(listing, (jnp.arange(top)[None, :] + rotation) % top, axis=1)


def portions_of(count, total, reach, skew, full):
    weights = [(1 << 20) // math.isqrt(grade ** skew) + 1 for grade in range(1, count + 1)]
    largest = reach if full else min(reach, max(-(-total // count), total * weights[0] // sum(weights)))
    least = 1 if total - largest >= count - 1 else 0
    given, rest = [largest] + [least] * (count - 1), total - largest - least * (count - 1)
    while rest > 0:
        free = [i for i in range(1, count) if given[i] < largest] or [i for i in range(1, count) if given[i] < reach]
        whole, budget = sum([weights[i] for i in free]), rest
        for i in free:
            extra = min(reach - given[i], max(1, budget * weights[i] // whole), rest)
            given[i] = given[i] + extra
            rest = rest - extra
    return np.array(given)


def noise(own_key, shape, scale, most, split=(), held_as=jnp.bfloat16):
    result = jax.random.normal(own_key, shape, jnp.float32) * scale
    if len(split) > 0:
        result = shard_levels(own_key, shape, split, -0.22, 0.18) * result
    return jnp.clip(result, min=-most, max=most).astype(held_as)


def setup_inputs(seed: int = 0) -> dict:
    arg_keys = jax.random.split(jax.random.key(seed), 13)
    state = noise(arg_keys[0], (NLON, NLAT, VARS, LEV), 1.0, 6.0, ((0, 4), (1, 8)), jnp.float32)
    diffusivity = jnp.clip(jnp.exp(jax.random.uniform(arg_keys[1], (VARS, LEV), jnp.float32, math.log(0.03), math.log(0.2))), 0.03, 0.2)
    wind = jnp.clip(jax.random.uniform(arg_keys[2], (NLON, NLAT), jnp.float32, -0.5, 0.5) * shard_levels(arg_keys[2], (NLON, NLAT), ((0, 4), (1, 8)), -0.4, 0.0), -0.5, 0.5)
    land_mask = set_ends((jax.random.randint(arg_keys[3], (NLON, NLAT), 0, 3) < 1).astype(jnp.int32), jax.random.fold_in(arg_keys[3], 1), 0, 1)
    routes_keys = jax.random.split(jax.random.fold_in(arg_keys[4], 1), N_TILE * N_LAT * N_EMU * COLS_DEV // COLS_DEV)
    routes_turns = jax.random.permutation(jax.random.fold_in(arg_keys[4], 3), N_TILE * N_LAT * N_EMU * COLS_DEV // COLS_DEV)
    routes = jax.vmap(lambda own, number: deal_out(jax.random.fold_in(arg_keys[4], 2), own, number, COLS_DEV, EXPERTS, 1, CAP, 2))(routes_keys, routes_turns).reshape((N_TILE, N_LAT, N_EMU, COLS_DEV, 1))
    counts = set_ends(jax.random.randint(arg_keys[5], (N_TILE, N_LAT, N_EMU), COLS_DEV // 4, COLS_DEV + 1), jax.random.fold_in(arg_keys[5], 1), COLS_DEV // 4, COLS_DEV).astype(jnp.int32)
    w_in = noise(arg_keys[6], (EXPERTS, VARS * LEV, HID), (VARS * LEV) ** -0.5, 0.15625, ((0, 16),))
    b_in = noise(arg_keys[7], (EXPERTS, HID), 0.5, 3.0, ((0, 16),), jnp.float32)
    land_vec = noise(arg_keys[8], (EXPERTS, HID), 1.0, 5.0, ((0, 16),), jnp.float32)
    w_hid = noise(arg_keys[9], (EXPERTS, LAYERS, HID, HID), HID ** -0.5, 0.1875, ((0, 16),))
    b_hid = noise(arg_keys[10], (EXPERTS, LAYERS, HID), 0.5, 3.0, ((0, 16),), jnp.float32)
    w_out = noise(arg_keys[11], (EXPERTS, HID, OUTV * LEV), HID ** -0.5, 0.1875, ((0, 16),))
    return {"state": state, "diffusivity": diffusivity, "wind": wind, "land_mask": land_mask, "routes": routes, "counts": counts, "w_in": w_in, "b_in": b_in, "land_vec": land_vec, "w_hid": w_hid, "b_hid": b_hid, "w_out": w_out}


def advance(center, east, west, north, south, diffusivity, wind):
    spread = east + west + north + south - 4.0 * center
    return center + diffusivity[None, None] * spread - 0.5 * wind[:, :, None, None] * (east - west)


def column_slots(route_flat, count, experts, capacity):
    columns = route_flat.shape[0]
    positions = jnp.arange(columns, dtype=jnp.int32)
    active = positions < count
    onehot = ((route_flat[:, None] == jnp.arange(experts, dtype=jnp.int32)[None, :]) & active[:, None]).astype(jnp.int32)
    before = jnp.cumsum(onehot, axis=0) - onehot
    ranking = jnp.sum(before * onehot, axis=1).astype(jnp.int32)
    slot_index = jnp.where(active, route_flat * capacity + ranking, experts * capacity)
    return slot_index.astype(jnp.int32), active


def run_network(features, flags, w_first, b_first, land_add, w_inner, b_inner, w_last):
    lead = features.shape[:-1]
    rows = features.reshape(-1, features.shape[-1])
    pre = jnp.dot(rows, w_first, preferred_element_type=jnp.float32) + b_first[None, :]
    pre = pre + flags.reshape(-1, 1).astype(jnp.float32) * land_add[None, :]
    hidden = jax.nn.silu(pre).astype(jnp.bfloat16)
    for number in range(w_inner.shape[0]):
        inner = jnp.dot(hidden, w_inner[number], preferred_element_type=jnp.float32) + b_inner[number][None, :]
        hidden = jax.nn.silu(inner).astype(jnp.bfloat16)
    produced = jnp.dot(hidden, w_last, preferred_element_type=jnp.float32).astype(jnp.bfloat16)
    return produced.reshape(lead + (w_last.shape[1],))


def place_rows(slot_index, values, experts, capacity):
    width = values.shape[-1]
    filled = jnp.zeros((experts * capacity + 1, width), values.dtype).at[slot_index].set(values)
    return filled[:-1].reshape(experts, capacity, width)


def pick_rows(slot_index, returned):
    width = returned.shape[-1]
    flat = jnp.concatenate([returned.reshape(-1, width), jnp.zeros((1, width), returned.dtype)], axis=0)
    return flat[slot_index]


def reference(state, diffusivity, wind, land_mask, routes, counts, w_in, b_in, land_vec, w_hid, b_hid, w_out):
    east = jnp.roll(state, -1, axis=0)
    west = jnp.roll(state, 1, axis=0)
    padded = jnp.pad(state, ((0, 0), (1, 1), (0, 0), (0, 0)))
    advanced = advance(state, east, west, padded[:, 2:], padded[:, :-2], diffusivity, wind)
    experts = N_TILE * N_LAT
    fsize = VARS * LEV
    columns = CLON * CLAT
    features = advanced.astype(jnp.bfloat16).reshape(N_TILE, CLON, N_LAT, N_EMU, CLAT, fsize)
    features = features.transpose(0, 2, 3, 1, 4, 5).reshape(experts, N_EMU, columns, fsize)
    land = land_mask.reshape(N_TILE, CLON, N_LAT, N_EMU, CLAT).transpose(0, 2, 3, 1, 4)
    land = land.reshape(experts, N_EMU, columns, 1).astype(jnp.bfloat16)
    route_cols = routes.reshape(experts, N_EMU, columns).astype(jnp.int32)
    count_dev = counts.reshape(experts, N_EMU).astype(jnp.int32)

    def slot_of(route_flat, count):
        return column_slots(route_flat, count, experts, CAP)[0]

    slot_index = jax.vmap(jax.vmap(slot_of))(route_cols, count_dev)

    def place(slots, values):
        return place_rows(slots, values, experts, CAP)

    outbound = jax.vmap(jax.vmap(place))(slot_index, features)
    flags = jax.vmap(jax.vmap(place))(slot_index, land)

    def serve(items):
        return run_network(items[0], items[1], items[2], items[3], items[4], items[5], items[6], items[7])

    produced = lax.map(serve, (jnp.moveaxis(outbound, 2, 0), jnp.moveaxis(flags, 2, 0), w_in, b_in, land_vec, w_hid, b_hid, w_out))
    returned = jnp.moveaxis(produced, 0, 2)
    tendency = jax.vmap(jax.vmap(pick_rows))(slot_index, returned).astype(jnp.float32)
    tendency = tendency.reshape(N_TILE, N_LAT, N_EMU, CLON, CLAT, OUTV, LEV).transpose(0, 3, 1, 2, 4, 5, 6)
    tendency = tendency.reshape(NLON, NLAT, OUTV, LEV)
    return advanced[:, :, :OUTV, :] + tendency
```

```python
import functools
import math

import jax
import jax.numpy as jnp
from jax import lax
from jax.experimental import pallas as pl
from jax.experimental.pallas import tpu as pltpu
from jax.sharding import PartitionSpec as P

F32 = jnp.float32
BF16 = jnp.bfloat16
VM = pl.BlockSpec(memory_space=pltpu.VMEM)
SM = pl.BlockSpec(memory_space=pltpu.SMEM)


class Plan:
    def __init__(self, experts, capacity):
        self.experts = experts
        self.full = capacity // 16 * 16
        self.rest = capacity - self.full
        self.group = 8 // math.gcd(self.rest, 8) if self.rest else 1
        self.chunk = self.group * self.rest

    def rows(self, variables):
        return variables * (self.full + self.rest)

    def spot(self, number, variables):
        return (number % self.group) * (variables // self.group) + number // self.group


def iota(shape, dim):
    return lax.broadcasted_iota(jnp.int32, shape, dim)


def hot(match):
    return jnp.where(match, 1.0, 0.0).astype(BF16)


def spread(plan, place):
    small, large = plan.experts * plan.rest, plan.experts * plan.chunk
    row = iota((small, large), 0)
    if plan.rest & (plan.rest - 1) == 0:
        source = lax.shift_right_logical(row, plan.rest.bit_length() - 1)
    else:
        source = lax.div(row, plan.rest)
    return row + source * (plan.chunk - plan.rest) + place * plan.rest, iota((small, large), 1)


def route_kernel(plan, count_ref, routes_ref, land_ref, wind_ref, *refs):
    refs = list(refs)
    flags_ref, wind_out = refs[:2]
    refs = refs[2:]
    column_ref = refs.pop()
    experts = plan.experts
    columns = routes_ref.shape[1]
    lons, lats = land_ref.shape
    routes = routes_ref[...]
    active = iota((1, columns), 1) < count_ref[0, 0]
    owner = (iota((experts, columns), 0) == routes) & active
    owner_hot = hot(owner)
    earlier = hot(iota((columns, columns), 0) < iota((columns, columns), 1))
    before = jnp.dot(owner_hot, earlier, preferred_element_type=F32)
    rank = jnp.sum(jnp.where(owner, before, 0.0), axis=0, keepdims=True)
    diagonal = iota((columns, columns), 0) == iota((columns, columns), 1)

    def upright(row):
        return jnp.sum(jnp.where(diagonal, row, 0.0), axis=1, keepdims=True)

    rank_int = rank.astype(jnp.int32)
    if plan.full:
        target = jnp.where(active & (rank_int < plan.full), routes * plan.full + rank_int, -1)
        total = experts * plan.full
        refs.pop(0)[...] = hot(iota((total, columns), 0) == target)
        tall = upright(target.astype(F32)).astype(jnp.int32)
        refs.pop(0)[...] = hot(iota((columns, total), 1) == tall)
    if plan.rest:
        pack_ref, pick_ref = refs.pop(0), refs.pop(0)
        total = experts * plan.chunk
        held = active & (rank_int >= plan.full)
        base = routes * plan.chunk + rank_int - plan.full
        for place in range(plan.group):
            target = jnp.where(held, base + place * plan.rest, -1)
            pack_ref[:, place * columns : (place + 1) * columns] = hot(
                iota((total, columns), 0) == target
            )
            tall = upright(target.astype(F32)).astype(jnp.int32)
            pick_ref[:, place * total : (place + 1) * total] = hot(
                iota((columns, total), 1) == tall
            )
    eye = iota((lats, lats), 0) == iota((lats, lats), 1)
    for lon in range(lons):
        rows = slice(lon * lats, (lon + 1) * lats)
        flag = jnp.where(eye, land_ref[lon : lon + 1, :].astype(F32), 0.0)
        column_ref[rows, :] = jnp.broadcast_to(
            jnp.sum(flag, axis=1, keepdims=True), (lats, column_ref.shape[1])
        )
        half = jnp.where(eye, 0.5 * wind_ref[lon : lon + 1, :], 0.0)
        wind_out[rows, :] = jnp.broadcast_to(
            jnp.sum(half, axis=1, keepdims=True), (lats, wind_out.shape[1])
        )
    lanes = flags_ref.shape[1]
    at = upright(rank).astype(jnp.int32) == iota((columns, lanes), 1)
    marked = jnp.where(at, column_ref[...], 0.0).astype(BF16)
    flags_ref[...] = jnp.dot(owner_hot, marked, preferred_element_type=F32)


def stencil_kernel(
    plan, state_ref, west_ref, east_ref, south_ref, north_ref, diff_ref, wind_ref, flags_ref, *refs
):
    refs = list(refs)
    pack_full = refs.pop(0) if plan.full else None
    pack_rest = refs.pop(0) if plan.rest else None
    out_ref, kept_ref, feature_ref = refs
    lons, variables, lats, levels = state_ref.shape
    columns = lons * lats
    kept = kept_ref.shape[1]
    row = iota((lats, levels), 0)
    for number in range(variables):
        spread_by = diff_ref[number : number + 1, :]
        spot = plan.spot(number, variables)
        for lon in range(lons):
            center = state_ref[lon, number]
            east = state_ref[lon + 1, number] if lon + 1 < lons else east_ref[number]
            west = state_ref[lon - 1, number] if lon else west_ref[number]
            north = jnp.where(
                row == lats - 1,
                north_ref[lon, number : number + 1, :],
                pltpu.roll(center, lats - 1, 0),
            )
            south = jnp.where(
                row == 0, south_ref[lon, number : number + 1, :], pltpu.roll(center, 1, 0)
            )
            total = east + west + north + south - 4.0 * center
            half = wind_ref[lon * lats : (lon + 1) * lats, :]
            moved = center + spread_by * total - half * (east - west)
            if number < kept:
                kept_ref[lon, number] = moved
            feature_ref[lon * lats : (lon + 1) * lats, spot * levels : (spot + 1) * levels] = (
                moved.astype(BF16)
            )
    experts = plan.experts
    if plan.full:
        packed = jnp.dot(pack_full[...], feature_ref[...], preferred_element_type=F32)
        for number in range(variables):
            spot = plan.spot(number, variables)
            block = packed[:, spot * levels : (spot + 1) * levels].astype(BF16)
            out_ref[:, number * plan.full : (number + 1) * plan.full, :] = block.reshape(
                experts, plan.full, levels
            )
    start = variables * plan.full
    if plan.rest:
        groups = variables // plan.group
        packed = jnp.zeros((experts * plan.chunk, groups * levels), F32)
        for place in range(plan.group):
            packed += jnp.dot(
                pack_rest[:, place * columns : (place + 1) * columns],
                feature_ref[:, place * groups * levels : (place + 1) * groups * levels],
                preferred_element_type=F32,
            )
        for group in range(groups):
            block = packed[:, group * levels : (group + 1) * levels]
            out_ref[:, start : start + plan.chunk, :] = block.reshape(
                experts, plan.chunk, levels
            ).astype(BF16)
            start += plan.chunk
    out_ref[:, start : start + 8, :] = jnp.broadcast_to(
        flags_ref[...].reshape(experts, 1, levels), (experts, 8, levels)
    ).astype(BF16)


def network_kernel(
    plan, rows_ref, w_first, b_first, land_add, w_inner, b_inner, w_last, out_ref, x_ref
):
    sources, _, levels = rows_ref.shape
    variables = w_first.shape[0] // levels
    lead = sources * plan.full
    small = sources * plan.rest
    marks = rows_ref[:, plan.rows(variables) :, :].astype(F32)
    flags = []
    if plan.full:
        for number in range(variables):
            block = rows_ref[:, number * plan.full : (number + 1) * plan.full, :]
            x_ref[:lead, number * levels : (number + 1) * levels] = block.reshape(lead, levels)
        tall = jnp.concatenate([marks] * (plan.full // 8), axis=1)
        match = iota(tall.shape, 1) == iota(tall.shape, 2)
        flags.append(jnp.sum(jnp.where(match, tall, 0.0), axis=2, keepdims=True).reshape(lead, 1))
    if plan.rest:
        start = variables * plan.full
        groups = variables // plan.group
        blocks = []
        for group in range(groups):
            block = rows_ref[:, start : start + plan.chunk, :].astype(F32)
            blocks.append(block.reshape(sources * plan.chunk, levels).astype(BF16))
            start += plan.chunk
        mixed = jnp.concatenate(blocks, axis=1)
        for place in range(plan.group):
            target, column = spread(plan, place)
            picked = jnp.dot(hot(target == column), mixed, preferred_element_type=F32)
            for group in range(groups):
                number = group * plan.group + place
                x_ref[lead:, number * levels : (number + 1) * levels] = picked[
                    :, group * levels : (group + 1) * levels
                ].astype(BF16)
        tall = jnp.concatenate([marks] * (plan.chunk // 8), axis=1)
        match = iota(tall.shape, 2) == iota(tall.shape, 1) + plan.full
        tall = jnp.sum(jnp.where(match, tall, 0.0), axis=2, keepdims=True)
        tall = jnp.broadcast_to(tall, (sources, plan.chunk, levels))
        tall = tall.reshape(sources * plan.chunk, levels).astype(BF16)
        target, column = spread(plan, 0)
        flags.append(jnp.dot(hot(target == column), tall, preferred_element_type=F32)[:, :1])
    flag = jnp.concatenate(flags, axis=0)
    pre = jnp.dot(x_ref[...], w_first[...], preferred_element_type=F32) + b_first[...]
    hidden = jax.nn.silu(pre + flag * land_add[...]).astype(BF16)
    for number in range(w_inner.shape[0]):
        pre = jnp.dot(hidden, w_inner[number], preferred_element_type=F32)
        hidden = jax.nn.silu(pre + b_inner[number : number + 1, :]).astype(BF16)
    made = jnp.dot(hidden, w_last[...], preferred_element_type=F32).astype(BF16)
    outs = made.shape[1] // levels
    if plan.full:
        for number in range(outs):
            block = made[:lead, number * levels : (number + 1) * levels]
            out_ref[:, number * plan.full : (number + 1) * plan.full, :] = block.reshape(
                sources, plan.full, levels
            )
    if plan.rest:
        start = outs * plan.full
        groups = outs // plan.group
        packed = jnp.zeros((sources * plan.chunk, groups * levels), F32)
        for place in range(plan.group):
            parts = [
                made[lead:, number * levels : (number + 1) * levels]
                for number in range(place, outs, plan.group)
            ]
            part = jnp.concatenate(parts, axis=1)
            target, column = spread(plan, place)
            packed += lax.dot_general(
                hot(target == column), part, (((0,), (0,)), ((), ())), preferred_element_type=F32
            )
        for group in range(groups):
            block = packed[:, group * levels : (group + 1) * levels]
            out_ref[:, start : start + plan.chunk, :] = block.reshape(
                sources, plan.chunk, levels
            ).astype(BF16)
            start += plan.chunk


def finish_kernel(plan, rows_ref, kept_ref, *refs):
    refs = list(refs)
    pick_full = refs.pop(0) if plan.full else None
    pick_rest = refs.pop(0) if plan.rest else None
    (out_ref,) = refs
    experts, _, levels = rows_ref.shape
    lons, outs, lats, _ = kept_ref.shape
    columns = lons * lats
    found = [None] * outs
    if plan.full:
        blocks = [
            rows_ref[:, number * plan.full : (number + 1) * plan.full, :].reshape(
                experts * plan.full, levels
            )
            for number in range(outs)
        ]
        full = jnp.dot(
            pick_full[...], jnp.concatenate(blocks, axis=1), preferred_element_type=F32
        )
        found = [full[:, number * levels : (number + 1) * levels] for number in range(outs)]
    if plan.rest:
        start = outs * plan.full
        groups = outs // plan.group
        total = experts * plan.chunk
        blocks = []
        for group in range(groups):
            block = rows_ref[:, start : start + plan.chunk, :].astype(F32)
            blocks.append(block.reshape(total, levels).astype(BF16))
            start += plan.chunk
        mixed = jnp.concatenate(blocks, axis=1)
        for place in range(plan.group):
            part = jnp.dot(
                pick_rest[:, place * total : (place + 1) * total],
                mixed,
                preferred_element_type=F32,
            )
            for group in range(groups):
                number = group * plan.group + place
                piece = part[:, group * levels : (group + 1) * levels]
                found[number] = piece if found[number] is None else found[number] + piece
    for number in range(outs):
        base = kept_ref[:, number].reshape(columns, levels)
        out_ref[pl.ds(number, columns, stride=outs), :] = base + found[number]


def call(kernel, specs, shapes, scratch=()):
    return pl.pallas_call(
        kernel,
        in_specs=specs,
        out_specs=jax.tree.map(lambda _: VM, shapes),
        out_shape=shapes,
        scratch_shapes=list(scratch),
        compiler_params=pltpu.CompilerParams(vmem_limit_bytes=48 * 1024 * 1024),
    )


def shape(dims, dtype):
    return jax.ShapeDtypeStruct(tuple(dims), dtype)


def exchanged(state):
    tiles = lax.axis_size("tile")
    bands = lax.axis_size("lat") * lax.axis_size("emu")
    up = [(i, (i + 1) % tiles) for i in range(tiles)]
    west = lax.ppermute(state[-1], "tile", up)
    east = lax.ppermute(state[0], "tile", [(b, a) for a, b in up])
    along = [(i, i + 1) for i in range(bands - 1)]
    south = lax.ppermute(state[:, :, -1, :], ("lat", "emu"), along)
    north = lax.ppermute(state[:, :, 0, :], ("lat", "emu"), [(b, a) for a, b in along])
    return west, east, south, north


def body(
    state, diffusivity, wind, land_mask, routes, counts, w_in, b_in, land_vec, w_hid, b_hid, w_out
):
    lons, lats, variables, levels = state.shape
    columns = lons * lats
    outs = w_out.shape[2] // levels
    experts = lax.axis_size("tile") * lax.axis_size("lat")
    capacity = max(2, columns * 5 // (4 * experts))
    plan = Plan(experts, capacity)
    state = jnp.transpose(state, (0, 2, 1, 3))
    halos = exchanged(state)

    shapes = [shape((experts, levels), F32), shape((columns, levels), F32)]
    if plan.full:
        total = experts * plan.full
        shapes += [shape((total, columns), BF16), shape((columns, total), BF16)]
    if plan.rest:
        total = experts * plan.chunk
        shapes += [
            shape((total, plan.group * columns), BF16),
            shape((columns, plan.group * total), BF16),
        ]
    made = call(
        functools.partial(route_kernel, plan),
        [SM, VM, VM, VM],
        shapes,
        [pltpu.VMEM((columns, levels), F32)],
    )(counts.reshape(1, 1), routes.reshape(1, columns), land_mask, wind)
    flags, half_wind = made[:2]
    packs, picks = made[2::2], made[3::2]

    rows, kept = call(
        functools.partial(stencil_kernel, plan),
        [VM] * (8 + len(packs)),
        [
            shape((experts, plan.rows(variables) + 8, levels), BF16),
            shape((lons, outs, lats, levels), F32),
        ],
        [pltpu.VMEM((columns, variables * levels), BF16)],
    )(state, *halos, diffusivity, half_wind, flags, *packs)

    axes = ("tile", "lat")
    rows = lax.all_to_all(rows, axes, split_axis=0, concat_axis=0, tiled=True)
    made = call(
        functools.partial(network_kernel, plan),
        [VM] * 7,
        shape((experts, plan.rows(outs), levels), BF16),
        [pltpu.VMEM((experts * capacity, variables * levels), BF16)],
    )(rows, w_in[0], b_in, land_vec, w_hid[0], b_hid[0], w_out[0])
    made = lax.all_to_all(made, axes, split_axis=0, concat_axis=0, tiled=True)
    out = call(
        functools.partial(finish_kernel, plan),
        [VM] * (2 + len(picks)),
        shape((columns * outs, levels), F32),
    )(made, kept, *picks)
    return out.reshape(lons, lats, outs, levels)


def solution(mesh):
    in_specs = (
        P("tile", ("lat", "emu"), None, None),
        P(),
        P("tile", ("lat", "emu")),
        P("tile", ("lat", "emu")),
        P("tile", "lat", "emu", None, None),
        P("tile", "lat", "emu"),
        P(("tile", "lat"), None, None),
        P(("tile", "lat"), None),
        P(("tile", "lat"), None),
        P(("tile", "lat"), None, None, None),
        P(("tile", "lat"), None, None),
        P(("tile", "lat"), None, None),
    )
    out_specs = P("tile", ("lat", "emu"), None, None)
    return jax.shard_map(body, mesh=mesh, in_specs=in_specs, out_specs=out_specs, check_vma=False)
```

```python
import functools
import math

import jax
import jax.numpy as jnp
from jax import lax
from jax.experimental import pallas as pl
from jax.experimental.pallas import tpu as pltpu
from jax.sharding import PartitionSpec as P

F32 = jnp.float32
BF16 = jnp.bfloat16
FIRST_PARTS = 3
VM = pl.BlockSpec(memory_space=pltpu.VMEM)
SM = pl.BlockSpec(memory_space=pltpu.SMEM)
HB = pl.BlockSpec(memory_space=pltpu.HBM)


class Plan:
    def __init__(self, experts, capacity):
        self.experts = experts
        self.full = capacity // 16 * 16
        self.rest = capacity - self.full
        self.group = 8 // math.gcd(self.rest, 8) if self.rest else 1
        self.chunk = self.group * self.rest

    def rows(self, variables):
        return variables * (self.full + self.rest)

    def spot(self, number, variables):
        return (number % self.group) * (variables // self.group) + number // self.group


def iota(shape, dim):
    return lax.broadcasted_iota(jnp.int32, shape, dim)


def hot(match):
    return jnp.where(match, 1.0, 0.0).astype(BF16)


def spread(plan, place):
    small, large = plan.experts * plan.rest, plan.experts * plan.chunk
    row = iota((small, large), 0)
    if plan.rest & (plan.rest - 1) == 0:
        source = lax.shift_right_logical(row, plan.rest.bit_length() - 1)
    else:
        source = lax.div(row, plan.rest)
    return row + source * (plan.chunk - plan.rest) + place * plan.rest, iota((small, large), 1)


def route_kernel(plan, count_ref, routes_ref, land_ref, wind_ref, *refs):
    refs = list(refs)
    flags_ref, wind_out = refs[:2]
    refs = refs[2:]
    column_ref = refs.pop()
    experts = plan.experts
    columns = routes_ref.shape[1]
    lons, lats = land_ref.shape
    routes = routes_ref[...]
    active = iota((1, columns), 1) < count_ref[0, 0]
    owner = (iota((experts, columns), 0) == routes) & active
    owner_hot = hot(owner)
    earlier = hot(iota((columns, columns), 0) < iota((columns, columns), 1))
    before = jnp.dot(owner_hot, earlier, preferred_element_type=F32)
    rank = jnp.sum(jnp.where(owner, before, 0.0), axis=0, keepdims=True)
    diagonal = iota((columns, columns), 0) == iota((columns, columns), 1)

    def upright(row):
        return jnp.sum(jnp.where(diagonal, row, 0.0), axis=1, keepdims=True)

    rank_int = rank.astype(jnp.int32)
    if plan.full:
        target = jnp.where(active & (rank_int < plan.full), routes * plan.full + rank_int, -1)
        total = experts * plan.full
        refs.pop(0)[...] = hot(iota((total, columns), 0) == target)
        tall = upright(target.astype(F32)).astype(jnp.int32)
        refs.pop(0)[...] = hot(iota((columns, total), 1) == tall)
    if plan.rest:
        pack_ref, pick_ref = refs.pop(0), refs.pop(0)
        total = experts * plan.chunk
        held = active & (rank_int >= plan.full)
        base = routes * plan.chunk + rank_int - plan.full
        for place in range(plan.group):
            target = jnp.where(held, base + place * plan.rest, -1)
            pack_ref[:, place * columns : (place + 1) * columns] = hot(
                iota((total, columns), 0) == target
            )
            tall = upright(target.astype(F32)).astype(jnp.int32)
            pick_ref[:, place * total : (place + 1) * total] = hot(
                iota((columns, total), 1) == tall
            )
    eye = iota((lats, lats), 0) == iota((lats, lats), 1)
    for lon in range(lons):
        rows = slice(lon * lats, (lon + 1) * lats)
        flag = jnp.where(eye, land_ref[lon : lon + 1, :].astype(F32), 0.0)
        column_ref[rows, :] = jnp.broadcast_to(
            jnp.sum(flag, axis=1, keepdims=True), (lats, column_ref.shape[1])
        )
        half = jnp.where(eye, 0.5 * wind_ref[lon : lon + 1, :], 0.0)
        wind_out[rows, :] = jnp.broadcast_to(
            jnp.sum(half, axis=1, keepdims=True), (lats, wind_out.shape[1])
        )
    lanes = flags_ref.shape[1]
    at = upright(rank).astype(jnp.int32) == iota((columns, lanes), 1)
    marked = jnp.where(at, column_ref[...], 0.0).astype(BF16)
    flags_ref[...] = jnp.dot(owner_hot, marked, preferred_element_type=F32)


def band_place():
    number = lax.axis_index("lat") * lax.axis_size("emu") + lax.axis_index("emu")
    return lax.rem(number, 2) == 0


def edge_kernel(*refs):
    *refs, top_ref, bottom_ref, inner_ref, outer_ref, sems = refs
    half = len(refs) // 2
    copies = [
        pltpu.make_async_copy(source, target, sems.at[k])
        for k, (source, target) in enumerate(zip(refs[:half], refs[half:]))
    ]
    for copy in copies:
        copy.start()
    copies[0].wait()
    state_ref = refs[half]
    lats = state_ref.shape[2]
    top_ref[...] = state_ref[state_ref.shape[0] - 1]
    bottom_ref[...] = state_ref[0]
    first, last = state_ref[:, :, 0, :], state_ref[:, :, lats - 1, :]
    even = band_place()
    inner_ref[...] = jnp.where(even, last, first)
    outer_ref[...] = jnp.where(even, first, last)
    for copy in copies[1:]:
        copy.wait()


def stencil_kernel(
    plan, state_ref, west_ref, east_ref, inner_ref, outer_ref, diff_ref, wind_ref, flags_ref, *refs
):
    refs = list(refs)
    even = band_place()
    pack_full = refs.pop(0) if plan.full else None
    pack_rest = refs.pop(0) if plan.rest else None
    out_ref, kept_ref, feature_ref = refs
    lons, variables, lats, levels = state_ref.shape
    columns = lons * lats
    kept = kept_ref.shape[1]
    row = iota((lats, levels), 0)
    for number in range(variables):
        spread_by = diff_ref[number : number + 1, :]
        spot = plan.spot(number, variables)
        for lon in range(lons):
            center = state_ref[lon, number]
            east = state_ref[lon + 1, number] if lon + 1 < lons else east_ref[number]
            west = state_ref[lon - 1, number] if lon else west_ref[number]
            inner = inner_ref[lon, number : number + 1, :]
            outer = outer_ref[lon, number : number + 1, :]
            north = jnp.where(
                row == lats - 1,
                jnp.where(even, inner, outer),
                pltpu.roll(center, lats - 1, 0),
            )
            south = jnp.where(
                row == 0, jnp.where(even, outer, inner), pltpu.roll(center, 1, 0)
            )
            total = east + west + north + south - 4.0 * center
            half = wind_ref[lon * lats : (lon + 1) * lats, :]
            moved = center + spread_by * total - half * (east - west)
            if number < kept:
                kept_ref[lon, number] = moved
            feature_ref[lon * lats : (lon + 1) * lats, spot * levels : (spot + 1) * levels] = (
                moved.astype(BF16)
            )
    experts = plan.experts
    if plan.full:
        packed = jnp.dot(pack_full[...], feature_ref[...], preferred_element_type=F32)
        for number in range(variables):
            spot = plan.spot(number, variables)
            block = packed[:, spot * levels : (spot + 1) * levels].astype(BF16)
            out_ref[:, number * plan.full : (number + 1) * plan.full, :] = block.reshape(
                experts, plan.full, levels
            )
    start = variables * plan.full
    if plan.rest:
        groups = variables // plan.group
        packed = jnp.zeros((experts * plan.chunk, groups * levels), F32)
        for place in range(plan.group):
            packed += jnp.dot(
                pack_rest[:, place * columns : (place + 1) * columns],
                feature_ref[:, place * groups * levels : (place + 1) * groups * levels],
                preferred_element_type=F32,
            )
        for group in range(groups):
            block = packed[:, group * levels : (group + 1) * levels]
            out_ref[:, start : start + plan.chunk, :] = block.reshape(
                experts, plan.chunk, levels
            ).astype(BF16)
            start += plan.chunk
    out_ref[:, start : start + 8, :] = jnp.broadcast_to(
        flags_ref[...].reshape(experts, 1, levels), (experts, 8, levels)
    ).astype(BF16)


def network_kernel(
    plan,
    rows_ref,
    b_first,
    land_add,
    b_inner,
    first_hbm,
    inner_hbm,
    last_hbm,
    out_ref,
    x_ref,
    w_first,
    w_inner,
    w_last,
    sems,
):
    sources, _, levels = rows_ref.shape
    step = w_first.shape[0] // FIRST_PARTS
    parts = [slice(k * step, (k + 1) * step) for k in range(FIRST_PARTS)]
    pairs = [(first_hbm.at[part], w_first.at[part]) for part in parts]
    pairs += [(inner_hbm.at[k], w_inner.at[k]) for k in range(w_inner.shape[0])]
    pairs += [(last_hbm, w_last)]
    copies = [
        pltpu.make_async_copy(source, target, sems.at[k])
        for k, (source, target) in enumerate(pairs)
    ]
    for copy in copies:
        copy.start()
    copies.reverse()
    variables = w_first.shape[0] // levels
    lead = sources * plan.full
    small = sources * plan.rest
    marks = rows_ref[:, plan.rows(variables) :, :].astype(F32)
    flags = []
    if plan.full:
        for number in range(variables):
            block = rows_ref[:, number * plan.full : (number + 1) * plan.full, :]
            x_ref[:lead, number * levels : (number + 1) * levels] = block.reshape(lead, levels)
        tall = jnp.concatenate([marks] * (plan.full // 8), axis=1)
        match = iota(tall.shape, 1) == iota(tall.shape, 2)
        flags.append(jnp.sum(jnp.where(match, tall, 0.0), axis=2, keepdims=True).reshape(lead, 1))
    if plan.rest:
        start = variables * plan.full
        groups = variables // plan.group
        blocks = []
        for group in range(groups):
            block = rows_ref[:, start : start + plan.chunk, :].astype(F32)
            blocks.append(block.reshape(sources * plan.chunk, levels).astype(BF16))
            start += plan.chunk
        mixed = jnp.concatenate(blocks, axis=1)
        for place in range(plan.group):
            target, column = spread(plan, place)
            picked = jnp.dot(hot(target == column), mixed, preferred_element_type=F32)
            for group in range(groups):
                number = group * plan.group + place
                x_ref[lead:, number * levels : (number + 1) * levels] = picked[
                    :, group * levels : (group + 1) * levels
                ].astype(BF16)
        tall = jnp.concatenate([marks] * (plan.chunk // 8), axis=1)
        match = iota(tall.shape, 2) == iota(tall.shape, 1) + plan.full
        tall = jnp.sum(jnp.where(match, tall, 0.0), axis=2, keepdims=True)
        tall = jnp.broadcast_to(tall, (sources, plan.chunk, levels))
        tall = tall.reshape(sources * plan.chunk, levels).astype(BF16)
        target, column = spread(plan, 0)
        flags.append(jnp.dot(hot(target == column), tall, preferred_element_type=F32)[:, :1])
    flag = jnp.concatenate(flags, axis=0)
    pre = jnp.broadcast_to(b_first[...], (x_ref.shape[0], b_first.shape[1]))
    for part in parts:
        copies.pop().wait()
        pre += jnp.dot(x_ref[:, part], w_first[part, :], preferred_element_type=F32)
    hidden = jax.nn.silu(pre + flag * land_add[...]).astype(BF16)
    for number in range(w_inner.shape[0]):
        copies.pop().wait()
        pre = jnp.dot(hidden, w_inner[number], preferred_element_type=F32)
        hidden = jax.nn.silu(pre + b_inner[number : number + 1, :]).astype(BF16)
    copies.pop().wait()
    made = jnp.dot(hidden, w_last[...], preferred_element_type=F32).astype(BF16)
    outs = made.shape[1] // levels
    if plan.full:
        for number in range(outs):
            block = made[:lead, number * levels : (number + 1) * levels]
            out_ref[:, number * plan.full : (number + 1) * plan.full, :] = block.reshape(
                sources, plan.full, levels
            )
    if plan.rest:
        start = outs * plan.full
        groups = outs // plan.group
        packed = jnp.zeros((sources * plan.chunk, groups * levels), F32)
        for place in range(plan.group):
            parts = [
                made[lead:, number * levels : (number + 1) * levels]
                for number in range(place, outs, plan.group)
            ]
            part = jnp.concatenate(parts, axis=1)
            target, column = spread(plan, place)
            packed += lax.dot_general(
                hot(target == column), part, (((0,), (0,)), ((), ())), preferred_element_type=F32
            )
        for group in range(groups):
            block = packed[:, group * levels : (group + 1) * levels]
            out_ref[:, start : start + plan.chunk, :] = block.reshape(
                sources, plan.chunk, levels
            ).astype(BF16)
            start += plan.chunk


def finish_kernel(plan, rows_ref, kept_ref, *refs):
    refs = list(refs)
    pick_full = refs.pop(0) if plan.full else None
    pick_rest = refs.pop(0) if plan.rest else None
    (out_ref,) = refs
    experts, _, levels = rows_ref.shape
    lons, outs, lats, _ = kept_ref.shape
    columns = lons * lats
    found = [None] * outs
    if plan.full:
        blocks = [
            rows_ref[:, number * plan.full : (number + 1) * plan.full, :].reshape(
                experts * plan.full, levels
            )
            for number in range(outs)
        ]
        full = jnp.dot(
            pick_full[...], jnp.concatenate(blocks, axis=1), preferred_element_type=F32
        )
        found = [full[:, number * levels : (number + 1) * levels] for number in range(outs)]
    if plan.rest:
        start = outs * plan.full
        groups = outs // plan.group
        total = experts * plan.chunk
        blocks = []
        for group in range(groups):
            block = rows_ref[:, start : start + plan.chunk, :].astype(F32)
            blocks.append(block.reshape(total, levels).astype(BF16))
            start += plan.chunk
        mixed = jnp.concatenate(blocks, axis=1)
        for place in range(plan.group):
            part = jnp.dot(
                pick_rest[:, place * total : (place + 1) * total],
                mixed,
                preferred_element_type=F32,
            )
            for group in range(groups):
                number = group * plan.group + place
                piece = part[:, group * levels : (group + 1) * levels]
                found[number] = piece if found[number] is None else found[number] + piece
    for number in range(outs):
        base = kept_ref[:, number].reshape(columns, levels)
        out_ref[pl.ds(number, columns, stride=outs), :] = base + found[number]


def call(kernel, specs, shapes, scratch=(), room=12):
    return pl.pallas_call(
        kernel,
        in_specs=specs,
        out_specs=jax.tree.map(lambda _: VM, shapes),
        out_shape=shapes,
        scratch_shapes=list(scratch),
        compiler_params=pltpu.CompilerParams(vmem_limit_bytes=room * 1024 * 1024),
    )


def shape(dims, dtype):
    return jax.ShapeDtypeStruct(tuple(dims), dtype)


def far(values):
    return pltpu.with_memory_space_constraint(values, pltpu.HBM)


def exchanged(state, *others):
    lons, variables, lats, levels = state.shape
    lon_edge = shape((variables, lats, levels), F32)
    lat_edge = shape((lons, variables, levels), F32)
    values = (state,) + others
    *values, top, bottom, inner, outer = call(
        edge_kernel,
        [HB] * len(values),
        [shape(v.shape, v.dtype) for v in values] + [lon_edge, lon_edge, lat_edge, lat_edge],
        [pltpu.SemaphoreType.DMA((len(values),))],
    )(*[far(v) for v in values])
    tiles = lax.axis_size("tile")
    bands = lax.axis_size("lat") * lax.axis_size("emu")
    up = [(i, (i + 1) % tiles) for i in range(tiles)]

    def swap(values, start):
        pairs = [(i, i + 1) for i in range(start, bands - 1, 2)]
        return lax.ppermute(values, ("lat", "emu"), pairs + [(b, a) for a, b in pairs])

    west = lax.ppermute(top, "tile", up)
    east = lax.ppermute(bottom, "tile", [(b, a) for a, b in up])
    return values, (west, east, swap(inner, 0), swap(outer, 1))


def body(
    state, diffusivity, wind, land_mask, routes, counts, w_in, b_in, land_vec, w_hid, b_hid, w_out
):
    lons, lats, variables, levels = state.shape
    columns = lons * lats
    outs = w_out.shape[2] // levels
    experts = lax.axis_size("tile") * lax.axis_size("lat")
    capacity = max(2, columns * 5 // (4 * experts))
    plan = Plan(experts, capacity)
    state = jnp.transpose(state, (0, 2, 1, 3))
    (state, diffusivity, wind, land_mask, routes), halos = exchanged(
        state, diffusivity, wind, land_mask, routes.reshape(1, columns)
    )

    shapes = [shape((experts, levels), F32), shape((columns, levels), F32)]
    if plan.full:
        total = experts * plan.full
        shapes += [shape((total, columns), BF16), shape((columns, total), BF16)]
    if plan.rest:
        total = experts * plan.chunk
        shapes += [
            shape((total, plan.group * columns), BF16),
            shape((columns, plan.group * total), BF16),
        ]
    made = call(
        functools.partial(route_kernel, plan),
        [SM, VM, VM, VM],
        shapes,
        [pltpu.VMEM((columns, levels), F32)],
    )(counts.reshape(1, 1), routes, land_mask, wind)
    flags, half_wind = made[:2]
    packs, picks = made[2::2], made[3::2]

    rows, kept = call(
        functools.partial(stencil_kernel, plan),
        [VM] * (8 + len(packs)),
        [
            shape((experts, plan.rows(variables) + 8, levels), BF16),
            shape((lons, outs, lats, levels), F32),
        ],
        [pltpu.VMEM((columns, variables * levels), BF16)],
    )(state, *halos, diffusivity, half_wind, flags, *packs)

    axes = ("tile", "lat")
    rows = lax.all_to_all(rows, axes, split_axis=0, concat_axis=0, tiled=True)
    made = call(
        functools.partial(network_kernel, plan),
        [VM] * 4 + [HB] * 3,
        shape((experts, plan.rows(outs), levels), BF16),
        [
            pltpu.VMEM((experts * capacity, variables * levels), BF16),
            pltpu.VMEM(w_in.shape[1:], BF16),
            pltpu.VMEM(w_hid.shape[1:], BF16),
            pltpu.VMEM(w_out.shape[1:], BF16),
            pltpu.SemaphoreType.DMA((FIRST_PARTS + w_hid.shape[1] + 1,)),
        ],
        32,
    )(rows, b_in, land_vec, b_hid[0], far(w_in[0]), far(w_hid[0]), far(w_out[0]))
    made = lax.all_to_all(made, axes, split_axis=0, concat_axis=0, tiled=True)
    out = call(
        functools.partial(finish_kernel, plan),
        [VM] * (2 + len(picks)),
        shape((columns * outs, levels), F32),
    )(made, kept, *picks)
    return out.reshape(lons, lats, outs, levels)


def solution(mesh):
    in_specs = (
        P("tile", ("lat", "emu"), None, None),
        P(),
        P("tile", ("lat", "emu")),
        P("tile", ("lat", "emu")),
        P("tile", "lat", "emu", None, None),
        P("tile", "lat", "emu"),
        P(("tile", "lat"), None, None),
        P(("tile", "lat"), None),
        P(("tile", "lat"), None),
        P(("tile", "lat"), None, None, None),
        P(("tile", "lat"), None, None),
        P(("tile", "lat"), None, None),
    )
    out_specs = P("tile", ("lat", "emu"), None, None)
    return jax.shard_map(body, mesh=mesh, in_specs=in_specs, out_specs=out_specs, check_vma=False)
```

```python
import functools
import math

import jax
import jax.numpy as jnp
from jax import lax
from jax.experimental import pallas as pl
from jax.experimental.pallas import tpu as pltpu
from jax.sharding import PartitionSpec as P

F32 = jnp.float32
BF16 = jnp.bfloat16
VM = pl.BlockSpec(memory_space=pltpu.VMEM)
SM = pl.BlockSpec(memory_space=pltpu.SMEM)
HB = pl.BlockSpec(memory_space=pltpu.HBM)


class Plan:
    def __init__(self, experts, capacity):
        self.experts = experts
        self.full = capacity // 16 * 16
        self.rest = capacity - self.full
        self.group = 8 // math.gcd(self.rest, 8) if self.rest else 1
        self.chunk = self.group * self.rest

    def rows(self, variables):
        return variables * (self.full + self.rest)

    def spot(self, number, variables):
        return (number % self.group) * (variables // self.group) + number // self.group


def iota(shape, dim):
    return lax.broadcasted_iota(jnp.int32, shape, dim)


def hot(match):
    return jnp.where(match, 1.0, 0.0).astype(BF16)


def spread(plan, place):
    small, large = plan.experts * plan.rest, plan.experts * plan.chunk
    row = iota((small, large), 0)
    if plan.rest & (plan.rest - 1) == 0:
        source = lax.shift_right_logical(row, plan.rest.bit_length() - 1)
    else:
        source = lax.div(row, plan.rest)
    return row + source * (plan.chunk - plan.rest) + place * plan.rest, iota((small, large), 1)


def route_kernel(plan, count_ref, routes_ref, land_ref, wind_ref, *refs):
    refs = list(refs)
    flags_ref, wind_out = refs[:2]
    refs = refs[2:]
    column_ref = refs.pop()
    experts = plan.experts
    columns = routes_ref.shape[1]
    lons, lats = land_ref.shape
    routes = routes_ref[...]
    active = iota((1, columns), 1) < count_ref[0, 0]
    owner = (iota((experts, columns), 0) == routes) & active
    owner_hot = hot(owner)
    earlier = hot(iota((columns, columns), 0) < iota((columns, columns), 1))
    before = jnp.dot(owner_hot, earlier, preferred_element_type=F32)
    rank = jnp.sum(jnp.where(owner, before, 0.0), axis=0, keepdims=True)
    diagonal = iota((columns, columns), 0) == iota((columns, columns), 1)

    def upright(row):
        return jnp.sum(jnp.where(diagonal, row, 0.0), axis=1, keepdims=True)

    rank_int = rank.astype(jnp.int32)
    if plan.full:
        target = jnp.where(active & (rank_int < plan.full), routes * plan.full + rank_int, -1)
        total = experts * plan.full
        refs.pop(0)[...] = hot(iota((total, columns), 0) == target)
        tall = upright(target.astype(F32)).astype(jnp.int32)
        refs.pop(0)[...] = hot(iota((columns, total), 1) == tall)
    if plan.rest:
        pack_ref, pick_ref = refs.pop(0), refs.pop(0)
        total = experts * plan.chunk
        held = active & (rank_int >= plan.full)
        base = routes * plan.chunk + rank_int - plan.full
        for place in range(plan.group):
            target = jnp.where(held, base + place * plan.rest, -1)
            pack_ref[:, place * columns : (place + 1) * columns] = hot(
                iota((total, columns), 0) == target
            )
            tall = upright(target.astype(F32)).astype(jnp.int32)
            pick_ref[:, place * total : (place + 1) * total] = hot(
                iota((columns, total), 1) == tall
            )
    eye = iota((lats, lats), 0) == iota((lats, lats), 1)
    for lon in range(lons):
        rows = slice(lon * lats, (lon + 1) * lats)
        flag = jnp.where(eye, land_ref[lon : lon + 1, :].astype(F32), 0.0)
        column_ref[rows, :] = jnp.broadcast_to(
            jnp.sum(flag, axis=1, keepdims=True), (lats, column_ref.shape[1])
        )
        half = jnp.where(eye, 0.5 * wind_ref[lon : lon + 1, :], 0.0)
        wind_out[rows, :] = jnp.broadcast_to(
            jnp.sum(half, axis=1, keepdims=True), (lats, wind_out.shape[1])
        )
    lanes = flags_ref.shape[1]
    at = upright(rank).astype(jnp.int32) == iota((columns, lanes), 1)
    marked = jnp.where(at, column_ref[...], 0.0).astype(BF16)
    flags_ref[...] = jnp.dot(owner_hot, marked, preferred_element_type=F32)


def band_place():
    number = lax.axis_index("lat") * lax.axis_size("emu") + lax.axis_index("emu")
    return lax.rem(number, 2) == 0


def edge_kernel(*refs):
    *refs, top_ref, bottom_ref, inner_ref, outer_ref, sems = refs
    half = len(refs) // 2
    copies = [
        pltpu.make_async_copy(source, target, sems.at[k])
        for k, (source, target) in enumerate(zip(refs[:half], refs[half:]))
    ]
    for copy in copies:
        copy.start()
    copies[0].wait()
    state_ref = refs[half]
    lats = state_ref.shape[2]
    top_ref[...] = state_ref[state_ref.shape[0] - 1]
    bottom_ref[...] = state_ref[0]
    first, last = state_ref[:, :, 0, :], state_ref[:, :, lats - 1, :]
    even = band_place()
    inner_ref[...] = jnp.where(even, last, first)
    outer_ref[...] = jnp.where(even, first, last)
    for copy in copies[1:]:
        copy.wait()


def stencil_kernel(
    plan, state_ref, west_ref, east_ref, inner_ref, outer_ref, diff_ref, wind_ref, flags_ref, *refs
):
    refs = list(refs)
    even = band_place()
    pack_full = refs.pop(0) if plan.full else None
    pack_rest = refs.pop(0) if plan.rest else None
    out_ref, kept_ref, feature_ref = refs
    lons, variables, lats, levels = state_ref.shape
    columns = lons * lats
    kept = kept_ref.shape[1]
    row = iota((lats, levels), 0)
    for number in range(variables):
        spread_by = diff_ref[number : number + 1, :]
        spot = plan.spot(number, variables)
        for lon in range(lons):
            center = state_ref[lon, number]
            east = state_ref[lon + 1, number] if lon + 1 < lons else east_ref[number]
            west = state_ref[lon - 1, number] if lon else west_ref[number]
            inner = inner_ref[lon, number : number + 1, :]
            outer = outer_ref[lon, number : number + 1, :]
            north = jnp.where(
                row == lats - 1,
                jnp.where(even, inner, outer),
                pltpu.roll(center, lats - 1, 0),
            )
            south = jnp.where(
                row == 0, jnp.where(even, outer, inner), pltpu.roll(center, 1, 0)
            )
            total = east + west + north + south - 4.0 * center
            half = wind_ref[lon * lats : (lon + 1) * lats, :]
            moved = center + spread_by * total - half * (east - west)
            if number < kept:
                kept_ref[lon, number] = moved
            feature_ref[lon * lats : (lon + 1) * lats, spot * levels : (spot + 1) * levels] = (
                moved.astype(BF16)
            )
    experts = plan.experts
    if plan.full:
        packed = jnp.dot(pack_full[...], feature_ref[...], preferred_element_type=F32)
        for number in range(variables):
            spot = plan.spot(number, variables)
            block = packed[:, spot * levels : (spot + 1) * levels].astype(BF16)
            out_ref[:, number * plan.full : (number + 1) * plan.full, :] = block.reshape(
                experts, plan.full, levels
            )
    start = variables * plan.full
    if plan.rest:
        groups = variables // plan.group
        packed = jnp.zeros((experts * plan.chunk, groups * levels), F32)
        for place in range(plan.group):
            packed += jnp.dot(
                pack_rest[:, place * columns : (place + 1) * columns],
                feature_ref[:, place * groups * levels : (place + 1) * groups * levels],
                preferred_element_type=F32,
            )
        for group in range(groups):
            block = packed[:, group * levels : (group + 1) * levels]
            out_ref[:, start : start + plan.chunk, :] = block.reshape(
                experts, plan.chunk, levels
            ).astype(BF16)
            start += plan.chunk
    out_ref[:, start : start + 8, :] = jnp.broadcast_to(
        flags_ref[...].reshape(experts, 1, levels), (experts, 8, levels)
    ).astype(BF16)


def network_kernel(
    plan,
    rows_ref,
    b_first,
    land_add,
    b_inner,
    w_first,
    inner_hbm,
    last_hbm,
    out_ref,
    x_ref,
    w_inner,
    w_last,
    sems,
):
    sources, _, levels = rows_ref.shape
    pairs = [(inner_hbm.at[k], w_inner.at[k]) for k in range(w_inner.shape[0])]
    pairs += [(last_hbm, w_last)]
    copies = [
        pltpu.make_async_copy(source, target, sems.at[k])
        for k, (source, target) in enumerate(pairs)
    ]
    for copy in copies:
        copy.start()
    copies.reverse()
    variables = w_first.shape[0] // levels
    lead = sources * plan.full
    small = sources * plan.rest
    marks = rows_ref[:, plan.rows(variables) :, :].astype(F32)
    flags = []
    if plan.full:
        for number in range(variables):
            block = rows_ref[:, number * plan.full : (number + 1) * plan.full, :]
            x_ref[:lead, number * levels : (number + 1) * levels] = block.reshape(lead, levels)
        tall = jnp.concatenate([marks] * (plan.full // 8), axis=1)
        match = iota(tall.shape, 1) == iota(tall.shape, 2)
        flags.append(jnp.sum(jnp.where(match, tall, 0.0), axis=2, keepdims=True).reshape(lead, 1))
    if plan.rest:
        start = variables * plan.full
        groups = variables // plan.group
        blocks = []
        for group in range(groups):
            block = rows_ref[:, start : start + plan.chunk, :].astype(F32)
            blocks.append(block.reshape(sources * plan.chunk, levels).astype(BF16))
            start += plan.chunk
        mixed = jnp.concatenate(blocks, axis=1)
        for place in range(plan.group):
            target, column = spread(plan, place)
            picked = jnp.dot(hot(target == column), mixed, preferred_element_type=F32)
            for group in range(groups):
                number = group * plan.group + place
                x_ref[lead:, number * levels : (number + 1) * levels] = picked[
                    :, group * levels : (group + 1) * levels
                ].astype(BF16)
        tall = jnp.concatenate([marks] * (plan.chunk // 8), axis=1)
        match = iota(tall.shape, 2) == iota(tall.shape, 1) + plan.full
        tall = jnp.sum(jnp.where(match, tall, 0.0), axis=2, keepdims=True)
        tall = jnp.broadcast_to(tall, (sources, plan.chunk, levels))
        tall = tall.reshape(sources * plan.chunk, levels).astype(BF16)
        target, column = spread(plan, 0)
        flags.append(jnp.dot(hot(target == column), tall, preferred_element_type=F32)[:, :1])
    flag = jnp.concatenate(flags, axis=0)
    pre = jnp.dot(x_ref[...], w_first[...], preferred_element_type=F32) + b_first[...]
    hidden = jax.nn.silu(pre + flag * land_add[...]).astype(BF16)
    for number in range(w_inner.shape[0]):
        copies.pop().wait()
        pre = jnp.dot(hidden, w_inner[number], preferred_element_type=F32)
        hidden = jax.nn.silu(pre + b_inner[number : number + 1, :]).astype(BF16)
    copies.pop().wait()
    made = jnp.dot(hidden, w_last[...], preferred_element_type=F32).astype(BF16)
    outs = made.shape[1] // levels
    if plan.full:
        for number in range(outs):
            block = made[:lead, number * levels : (number + 1) * levels]
            out_ref[:, number * plan.full : (number + 1) * plan.full, :] = block.reshape(
                sources, plan.full, levels
            )
    if plan.rest:
        start = outs * plan.full
        groups = outs // plan.group
        packed = jnp.zeros((sources * plan.chunk, groups * levels), F32)
        for place in range(plan.group):
            parts = [
                made[lead:, number * levels : (number + 1) * levels]
                for number in range(place, outs, plan.group)
            ]
            part = jnp.concatenate(parts, axis=1)
            target, column = spread(plan, place)
            packed += lax.dot_general(
                hot(target == column), part, (((0,), (0,)), ((), ())), preferred_element_type=F32
            )
        for group in range(groups):
            block = packed[:, group * levels : (group + 1) * levels]
            out_ref[:, start : start + plan.chunk, :] = block.reshape(
                sources, plan.chunk, levels
            ).astype(BF16)
            start += plan.chunk


def finish_kernel(plan, rows_ref, kept_ref, *refs):
    refs = list(refs)
    pick_full = refs.pop(0) if plan.full else None
    pick_rest = refs.pop(0) if plan.rest else None
    (out_ref,) = refs
    experts, _, levels = rows_ref.shape
    lons, outs, lats, _ = kept_ref.shape
    columns = lons * lats
    found = [None] * outs
    if plan.full:
        blocks = [
            rows_ref[:, number * plan.full : (number + 1) * plan.full, :].reshape(
                experts * plan.full, levels
            )
            for number in range(outs)
        ]
        full = jnp.dot(
            pick_full[...], jnp.concatenate(blocks, axis=1), preferred_element_type=F32
        )
        found = [full[:, number * levels : (number + 1) * levels] for number in range(outs)]
    if plan.rest:
        start = outs * plan.full
        groups = outs // plan.group
        total = experts * plan.chunk
        blocks = []
        for group in range(groups):
            block = rows_ref[:, start : start + plan.chunk, :].astype(F32)
            blocks.append(block.reshape(total, levels).astype(BF16))
            start += plan.chunk
        mixed = jnp.concatenate(blocks, axis=1)
        for place in range(plan.group):
            part = jnp.dot(
                pick_rest[:, place * total : (place + 1) * total],
                mixed,
                preferred_element_type=F32,
            )
            for group in range(groups):
                number = group * plan.group + place
                piece = part[:, group * levels : (group + 1) * levels]
                found[number] = piece if found[number] is None else found[number] + piece
    for number in range(outs):
        base = kept_ref[:, number].reshape(columns, levels)
        out_ref[pl.ds(number, columns, stride=outs), :] = base + found[number]


def call(kernel, specs, shapes, scratch=(), room=12):
    return pl.pallas_call(
        kernel,
        in_specs=specs,
        out_specs=jax.tree.map(lambda _: VM, shapes),
        out_shape=shapes,
        scratch_shapes=list(scratch),
        compiler_params=pltpu.CompilerParams(vmem_limit_bytes=room * 1024 * 1024),
    )


def shape(dims, dtype):
    return jax.ShapeDtypeStruct(tuple(dims), dtype)


def far(values):
    return pltpu.with_memory_space_constraint(values, pltpu.HBM)


def exchanged(state, *others):
    lons, variables, lats, levels = state.shape
    lon_edge = shape((variables, lats, levels), F32)
    lat_edge = shape((lons, variables, levels), F32)
    values = (state,) + others
    *values, top, bottom, inner, outer = call(
        edge_kernel,
        [HB] * len(values),
        [shape(v.shape, v.dtype) for v in values] + [lon_edge, lon_edge, lat_edge, lat_edge],
        [pltpu.SemaphoreType.DMA((len(values),))],
    )(*[far(v) for v in values])
    tiles = lax.axis_size("tile")
    bands = lax.axis_size("lat") * lax.axis_size("emu")
    up = [(i, (i + 1) % tiles) for i in range(tiles)]

    def swap(values, start):
        pairs = [(i, i + 1) for i in range(start, bands - 1, 2)]
        return lax.ppermute(values, ("lat", "emu"), pairs + [(b, a) for a, b in pairs])

    outer = swap(outer, 1)
    west = lax.ppermute(top, "tile", up)
    east = lax.ppermute(bottom, "tile", [(b, a) for a, b in up])
    inner = swap(inner, 0)
    return values, (west, east, inner, outer)


def body(
    state, diffusivity, wind, land_mask, routes, counts, w_in, b_in, land_vec, w_hid, b_hid, w_out
):
    lons, lats, variables, levels = state.shape
    columns = lons * lats
    outs = w_out.shape[2] // levels
    experts = lax.axis_size("tile") * lax.axis_size("lat")
    capacity = max(2, columns * 5 // (4 * experts))
    plan = Plan(experts, capacity)
    state = jnp.transpose(state, (0, 2, 1, 3))
    (state, diffusivity, wind, land_mask, routes), halos = exchanged(
        state, diffusivity, wind, land_mask, routes.reshape(1, columns)
    )

    shapes = [shape((experts, levels), F32), shape((columns, levels), F32)]
    if plan.full:
        total = experts * plan.full
        shapes += [shape((total, columns), BF16), shape((columns, total), BF16)]
    if plan.rest:
        total = experts * plan.chunk
        shapes += [
            shape((total, plan.group * columns), BF16),
            shape((columns, plan.group * total), BF16),
        ]
    made = call(
        functools.partial(route_kernel, plan),
        [SM, VM, VM, VM],
        shapes,
        [pltpu.VMEM((columns, levels), F32)],
    )(counts.reshape(1, 1), routes, land_mask, wind)
    flags, half_wind = made[:2]
    packs, picks = made[2::2], made[3::2]

    rows, kept = call(
        functools.partial(stencil_kernel, plan),
        [VM] * (8 + len(packs)),
        [
            shape((experts, plan.rows(variables) + 8, levels), BF16),
            shape((lons, outs, lats, levels), F32),
        ],
        [pltpu.VMEM((columns, variables * levels), BF16)],
    )(state, *halos, diffusivity, half_wind, flags, *packs)

    axes = ("tile", "lat")
    rows = lax.all_to_all(rows, axes, split_axis=0, concat_axis=0, tiled=True)
    made = call(
        functools.partial(network_kernel, plan),
        [VM] * 5 + [HB] * 2,
        shape((experts, plan.rows(outs), levels), BF16),
        [
            pltpu.VMEM((experts * capacity, variables * levels), BF16),
            pltpu.VMEM(w_hid.shape[1:], BF16),
            pltpu.VMEM(w_out.shape[1:], BF16),
            pltpu.SemaphoreType.DMA((w_hid.shape[1] + 1,)),
        ],
        32,
    )(rows, b_in, land_vec, b_hid[0], w_in[0], far(w_hid[0]), far(w_out[0]))
    made = lax.all_to_all(made, axes, split_axis=0, concat_axis=0, tiled=True)
    out = call(
        functools.partial(finish_kernel, plan),
        [VM] * (2 + len(picks)),
        shape((columns * outs, levels), F32),
    )(made, kept, *picks)
    return out.reshape(lons, lats, outs, levels)


def solution(mesh):
    in_specs = (
        P("tile", ("lat", "emu"), None, None),
        P(),
        P("tile", ("lat", "emu")),
        P("tile", ("lat", "emu")),
        P("tile", "lat", "emu", None, None),
        P("tile", "lat", "emu"),
        P(("tile", "lat"), None, None),
        P(("tile", "lat"), None),
        P(("tile", "lat"), None),
        P(("tile", "lat"), None, None, None),
        P(("tile", "lat"), None, None),
        P(("tile", "lat"), None, None),
    )
    out_specs = P("tile", ("lat", "emu"), None, None)
    return jax.shard_map(body, mesh=mesh, in_specs=in_specs, out_specs=out_specs, check_vma=False)
```

```python
import functools
import math

import jax
import jax.numpy as jnp
from jax import lax
from jax.experimental import pallas as pl
from jax.experimental.pallas import tpu as pltpu
from jax.sharding import PartitionSpec as P

F32 = jnp.float32
BF16 = jnp.bfloat16
VM = pl.BlockSpec(memory_space=pltpu.VMEM)
SM = pl.BlockSpec(memory_space=pltpu.SMEM)
HB = pl.BlockSpec(memory_space=pltpu.HBM)


class Plan:
    def __init__(self, experts, capacity):
        self.experts = experts
        self.full = capacity // 16 * 16
        self.rest = capacity - self.full
        self.group = 8 // math.gcd(self.rest, 8) if self.rest else 1
        self.chunk = self.group * self.rest

    def rows(self, variables):
        return variables * (self.full + self.rest)

    def spot(self, number, variables):
        return (number % self.group) * (variables // self.group) + number // self.group


def iota(shape, dim):
    return lax.broadcasted_iota(jnp.int32, shape, dim)


def hot(match):
    return jnp.where(match, 1.0, 0.0).astype(BF16)


def spread(plan, place):
    small, large = plan.experts * plan.rest, plan.experts * plan.chunk
    row = iota((small, large), 0)
    if plan.rest & (plan.rest - 1) == 0:
        source = lax.shift_right_logical(row, plan.rest.bit_length() - 1)
    else:
        source = lax.div(row, plan.rest)
    return row + source * (plan.chunk - plan.rest) + place * plan.rest, iota((small, large), 1)


def route_kernel(plan, count_ref, routes_ref, land_ref, wind_ref, *refs):
    refs = list(refs)
    flags_ref, wind_out = refs[:2]
    refs = refs[2:]
    column_ref = refs.pop()
    experts = plan.experts
    columns = routes_ref.shape[1]
    lons, lats = land_ref.shape
    routes = routes_ref[...]
    active = iota((1, columns), 1) < count_ref[0, 0]
    owner = (iota((experts, columns), 0) == routes) & active
    owner_hot = hot(owner)
    earlier = hot(iota((columns, columns), 0) < iota((columns, columns), 1))
    before = jnp.dot(owner_hot, earlier, preferred_element_type=F32)
    rank = jnp.sum(jnp.where(owner, before, 0.0), axis=0, keepdims=True)
    diagonal = iota((columns, columns), 0) == iota((columns, columns), 1)

    def upright(row):
        return jnp.sum(jnp.where(diagonal, row, 0.0), axis=1, keepdims=True)

    rank_int = rank.astype(jnp.int32)
    if plan.full:
        target = jnp.where(active & (rank_int < plan.full), routes * plan.full + rank_int, -1)
        total = experts * plan.full
        refs.pop(0)[...] = hot(iota((total, columns), 0) == target)
        tall = upright(target.astype(F32)).astype(jnp.int32)
        refs.pop(0)[...] = hot(iota((columns, total), 1) == tall)
    if plan.rest:
        pack_ref, pick_ref = refs.pop(0), refs.pop(0)
        total = experts * plan.chunk
        held = active & (rank_int >= plan.full)
        base = routes * plan.chunk + rank_int - plan.full
        for place in range(plan.group):
            target = jnp.where(held, base + place * plan.rest, -1)
            pack_ref[:, place * columns : (place + 1) * columns] = hot(
                iota((total, columns), 0) == target
            )
            tall = upright(target.astype(F32)).astype(jnp.int32)
            pick_ref[:, place * total : (place + 1) * total] = hot(
                iota((columns, total), 1) == tall
            )
    eye = iota((lats, lats), 0) == iota((lats, lats), 1)
    for lon in range(lons):
        rows = slice(lon * lats, (lon + 1) * lats)
        flag = jnp.where(eye, land_ref[lon : lon + 1, :].astype(F32), 0.0)
        column_ref[rows, :] = jnp.broadcast_to(
            jnp.sum(flag, axis=1, keepdims=True), (lats, column_ref.shape[1])
        )
        half = jnp.where(eye, 0.5 * wind_ref[lon : lon + 1, :], 0.0)
        wind_out[rows, :] = jnp.broadcast_to(
            jnp.sum(half, axis=1, keepdims=True), (lats, wind_out.shape[1])
        )
    lanes = flags_ref.shape[1]
    at = upright(rank).astype(jnp.int32) == iota((columns, lanes), 1)
    marked = jnp.where(at, column_ref[...], 0.0).astype(BF16)
    flags_ref[...] = jnp.dot(owner_hot, marked, preferred_element_type=F32)


def band_place():
    number = lax.axis_index("lat") * lax.axis_size("emu") + lax.axis_index("emu")
    return lax.rem(number, 2) == 0


def edge_kernel(*refs):
    *refs, outer_ref, top_ref, bottom_ref, inner_ref, sems = refs
    half = len(refs) // 2
    copies = [
        pltpu.make_async_copy(source, target, sems.at[k])
        for k, (source, target) in enumerate(zip(refs[:half], refs[half:]))
    ]
    for copy in copies:
        copy.start()
    copies[0].wait()
    state_ref = refs[half]
    lats = state_ref.shape[2]
    top_ref[...] = state_ref[state_ref.shape[0] - 1].astype(BF16)
    bottom_ref[...] = state_ref[0].astype(BF16)
    first, last = state_ref[:, :, 0, :], state_ref[:, :, lats - 1, :]
    even = band_place()
    inner_ref[...] = jnp.where(even, last, first).astype(BF16)
    outer_ref[...] = jnp.where(even, first, last).astype(BF16)
    for copy in copies[1:]:
        copy.wait()


def stencil_kernel(
    plan, state_ref, outer_ref, west_ref, east_ref, inner_ref, diff_ref, wind_ref, flags_ref, *refs
):
    refs = list(refs)
    even = band_place()
    pack_full = refs.pop(0) if plan.full else None
    pack_rest = refs.pop(0) if plan.rest else None
    out_ref, kept_ref, feature_ref = refs
    lons, variables, lats, levels = state_ref.shape
    columns = lons * lats
    kept = kept_ref.shape[1]
    row = iota((lats, levels), 0)
    inner_rows, outer_rows = inner_ref[...].astype(F32), outer_ref[...].astype(F32)
    for number in range(variables):
        spread_by = diff_ref[number : number + 1, :]
        spot = plan.spot(number, variables)
        for lon in range(lons):
            center = state_ref[lon, number]
            east = state_ref[lon + 1, number] if lon + 1 < lons else east_ref[number].astype(F32)
            west = state_ref[lon - 1, number] if lon else west_ref[number].astype(F32)
            inner = inner_rows[lon, number : number + 1, :]
            outer = outer_rows[lon, number : number + 1, :]
            north = jnp.where(
                row == lats - 1,
                jnp.where(even, inner, outer),
                pltpu.roll(center, lats - 1, 0),
            )
            south = jnp.where(
                row == 0, jnp.where(even, outer, inner), pltpu.roll(center, 1, 0)
            )
            total = east + west + north + south - 4.0 * center
            half = wind_ref[lon * lats : (lon + 1) * lats, :]
            moved = center + spread_by * total - half * (east - west)
            if number < kept:
                kept_ref[lon, number] = moved
            feature_ref[lon * lats : (lon + 1) * lats, spot * levels : (spot + 1) * levels] = (
                moved.astype(BF16)
            )
    experts = plan.experts
    if plan.full:
        packed = jnp.dot(pack_full[...], feature_ref[...], preferred_element_type=F32)
        for number in range(variables):
            spot = plan.spot(number, variables)
            block = packed[:, spot * levels : (spot + 1) * levels].astype(BF16)
            out_ref[:, number * plan.full : (number + 1) * plan.full, :] = block.reshape(
                experts, plan.full, levels
            )
    start = variables * plan.full
    if plan.rest:
        groups = variables // plan.group
        packed = jnp.zeros((experts * plan.chunk, groups * levels), F32)
        for place in range(plan.group):
            packed += jnp.dot(
                pack_rest[:, place * columns : (place + 1) * columns],
                feature_ref[:, place * groups * levels : (place + 1) * groups * levels],
                preferred_element_type=F32,
            )
        for group in range(groups):
            block = packed[:, group * levels : (group + 1) * levels]
            out_ref[:, start : start + plan.chunk, :] = block.reshape(
                experts, plan.chunk, levels
            ).astype(BF16)
            start += plan.chunk
    out_ref[:, start : start + 8, :] = jnp.broadcast_to(
        flags_ref[...].reshape(experts, 1, levels), (experts, 8, levels)
    ).astype(BF16)


def network_kernel(
    plan,
    rows_ref,
    b_first,
    land_add,
    b_inner,
    w_first,
    inner_hbm,
    last_hbm,
    out_ref,
    x_ref,
    w_inner,
    w_last,
    sems,
):
    sources, _, levels = rows_ref.shape
    pairs = [(inner_hbm.at[k], w_inner.at[k]) for k in range(w_inner.shape[0])]
    pairs += [(last_hbm, w_last)]
    copies = [
        pltpu.make_async_copy(source, target, sems.at[k])
        for k, (source, target) in enumerate(pairs)
    ]
    for copy in copies:
        copy.start()
    copies.reverse()
    variables = w_first.shape[0] // levels
    lead = sources * plan.full
    small = sources * plan.rest
    marks = rows_ref[:, plan.rows(variables) :, :].astype(F32)
    flags = []
    if plan.full:
        for number in range(variables):
            block = rows_ref[:, number * plan.full : (number + 1) * plan.full, :]
            x_ref[:lead, number * levels : (number + 1) * levels] = block.reshape(lead, levels)
        tall = jnp.concatenate([marks] * (plan.full // 8), axis=1)
        match = iota(tall.shape, 1) == iota(tall.shape, 2)
        flags.append(jnp.sum(jnp.where(match, tall, 0.0), axis=2, keepdims=True).reshape(lead, 1))
    if plan.rest:
        start = variables * plan.full
        groups = variables // plan.group
        blocks = []
        for group in range(groups):
            block = rows_ref[:, start : start + plan.chunk, :].astype(F32)
            blocks.append(block.reshape(sources * plan.chunk, levels).astype(BF16))
            start += plan.chunk
        mixed = jnp.concatenate(blocks, axis=1)
        for place in range(plan.group):
            target, column = spread(plan, place)
            picked = jnp.dot(hot(target == column), mixed, preferred_element_type=F32)
            for group in range(groups):
                number = group * plan.group + place
                x_ref[lead:, number * levels : (number + 1) * levels] = picked[
                    :, group * levels : (group + 1) * levels
                ].astype(BF16)
        tall = jnp.concatenate([marks] * (plan.chunk // 8), axis=1)
        match = iota(tall.shape, 2) == iota(tall.shape, 1) + plan.full
        tall = jnp.sum(jnp.where(match, tall, 0.0), axis=2, keepdims=True)
        tall = jnp.broadcast_to(tall, (sources, plan.chunk, levels))
        tall = tall.reshape(sources * plan.chunk, levels).astype(BF16)
        target, column = spread(plan, 0)
        flags.append(jnp.dot(hot(target == column), tall, preferred_element_type=F32)[:, :1])
    flag = jnp.concatenate(flags, axis=0)
    pre = jnp.dot(x_ref[...], w_first[...], preferred_element_type=F32) + b_first[...]
    hidden = jax.nn.silu(pre + flag * land_add[...]).astype(BF16)
    for number in range(w_inner.shape[0]):
        copies.pop().wait()
        pre = jnp.dot(hidden, w_inner[number], preferred_element_type=F32)
        hidden = jax.nn.silu(pre + b_inner[number : number + 1, :]).astype(BF16)
    copies.pop().wait()
    made = jnp.dot(hidden, w_last[...], preferred_element_type=F32).astype(BF16)
    outs = made.shape[1] // levels
    if plan.full:
        for number in range(outs):
            block = made[:lead, number * levels : (number + 1) * levels]
            out_ref[:, number * plan.full : (number + 1) * plan.full, :] = block.reshape(
                sources, plan.full, levels
            )
    if plan.rest:
        start = outs * plan.full
        groups = outs // plan.group
        packed = jnp.zeros((sources * plan.chunk, groups * levels), F32)
        for place in range(plan.group):
            parts = [
                made[lead:, number * levels : (number + 1) * levels]
                for number in range(place, outs, plan.group)
            ]
            part = jnp.concatenate(parts, axis=1)
            target, column = spread(plan, place)
            packed += lax.dot_general(
                hot(target == column), part, (((0,), (0,)), ((), ())), preferred_element_type=F32
            )
        for group in range(groups):
            block = packed[:, group * levels : (group + 1) * levels]
            out_ref[:, start : start + plan.chunk, :] = block.reshape(
                sources, plan.chunk, levels
            ).astype(BF16)
            start += plan.chunk


def finish_kernel(plan, rows_ref, kept_ref, *refs):
    refs = list(refs)
    pick_full = refs.pop(0) if plan.full else None
    pick_rest = refs.pop(0) if plan.rest else None
    (out_ref,) = refs
    experts, _, levels = rows_ref.shape
    lons, outs, lats, _ = kept_ref.shape
    columns = lons * lats
    found = [None] * outs
    if plan.full:
        blocks = [
            rows_ref[:, number * plan.full : (number + 1) * plan.full, :].reshape(
                experts * plan.full, levels
            )
            for number in range(outs)
        ]
        full = jnp.dot(
            pick_full[...], jnp.concatenate(blocks, axis=1), preferred_element_type=F32
        )
        found = [full[:, number * levels : (number + 1) * levels] for number in range(outs)]
    if plan.rest:
        start = outs * plan.full
        groups = outs // plan.group
        total = experts * plan.chunk
        blocks = []
        for group in range(groups):
            block = rows_ref[:, start : start + plan.chunk, :].astype(F32)
            blocks.append(block.reshape(total, levels).astype(BF16))
            start += plan.chunk
        mixed = jnp.concatenate(blocks, axis=1)
        for place in range(plan.group):
            part = jnp.dot(
                pick_rest[:, place * total : (place + 1) * total],
                mixed,
                preferred_element_type=F32,
            )
            for group in range(groups):
                number = group * plan.group + place
                piece = part[:, group * levels : (group + 1) * levels]
                found[number] = piece if found[number] is None else found[number] + piece
    for number in range(outs):
        base = kept_ref[:, number].reshape(columns, levels)
        out_ref[pl.ds(number, columns, stride=outs), :] = base + found[number]


def call(kernel, specs, shapes, scratch=(), room=12):
    return pl.pallas_call(
        kernel,
        in_specs=specs,
        out_specs=jax.tree.map(lambda _: VM, shapes),
        out_shape=shapes,
        scratch_shapes=list(scratch),
        compiler_params=pltpu.CompilerParams(vmem_limit_bytes=room * 1024 * 1024),
    )


def shape(dims, dtype):
    return jax.ShapeDtypeStruct(tuple(dims), dtype)


def far(values):
    return pltpu.with_memory_space_constraint(values, pltpu.HBM)


def exchanged(state, *others):
    lons, variables, lats, levels = state.shape
    lon_edge = shape((variables, lats, levels), BF16)
    lat_edge = shape((lons, variables, levels), BF16)
    values = (state,) + others
    *values, outer, top, bottom, inner = call(
        edge_kernel,
        [HB] * len(values),
        [shape(v.shape, v.dtype) for v in values] + [lat_edge, lon_edge, lon_edge, lat_edge],
        [pltpu.SemaphoreType.DMA((len(values),))],
    )(*[far(v) for v in values])
    tiles = lax.axis_size("tile")
    bands = lax.axis_size("lat") * lax.axis_size("emu")
    up = [(i, (i + 1) % tiles) for i in range(tiles)]

    def swap(values, start):
        pairs = [(i, i + 1) for i in range(start, bands - 1, 2)]
        return lax.ppermute(values, ("lat", "emu"), pairs + [(b, a) for a, b in pairs])

    outer = swap(outer, 1)
    west = lax.ppermute(top, "tile", up)
    east = lax.ppermute(bottom, "tile", [(b, a) for a, b in up])
    inner = swap(inner, 0)
    return values, (outer, west, east, inner)


def body(
    state, diffusivity, wind, land_mask, routes, counts, w_in, b_in, land_vec, w_hid, b_hid, w_out
):
    lons, lats, variables, levels = state.shape
    columns = lons * lats
    outs = w_out.shape[2] // levels
    experts = lax.axis_size("tile") * lax.axis_size("lat")
    capacity = max(2, columns * 5 // (4 * experts))
    plan = Plan(experts, capacity)
    state = jnp.transpose(state, (0, 2, 1, 3))
    (state, diffusivity, wind, land_mask, routes), halos = exchanged(
        state, diffusivity, wind, land_mask, routes.reshape(1, columns)
    )

    shapes = [shape((experts, levels), F32), shape((columns, levels), F32)]
    if plan.full:
        total = experts * plan.full
        shapes += [shape((total, columns), BF16), shape((columns, total), BF16)]
    if plan.rest:
        total = experts * plan.chunk
        shapes += [
            shape((total, plan.group * columns), BF16),
            shape((columns, plan.group * total), BF16),
        ]
    made = call(
        functools.partial(route_kernel, plan),
        [SM, VM, VM, VM],
        shapes,
        [pltpu.VMEM((columns, levels), F32)],
    )(counts.reshape(1, 1), routes, land_mask, wind)
    flags, half_wind = made[:2]
    packs, picks = made[2::2], made[3::2]

    rows, kept = call(
        functools.partial(stencil_kernel, plan),
        [VM] * (8 + len(packs)),
        [
            shape((experts, plan.rows(variables) + 8, levels), BF16),
            shape((lons, outs, lats, levels), F32),
        ],
        [pltpu.VMEM((columns, variables * levels), BF16)],
    )(state, *halos, diffusivity, half_wind, flags, *packs)

    axes = ("tile", "lat")
    rows = lax.all_to_all(rows, axes, split_axis=0, concat_axis=0, tiled=True)
    made = call(
        functools.partial(network_kernel, plan),
        [VM] * 5 + [HB] * 2,
        shape((experts, plan.rows(outs), levels), BF16),
        [
            pltpu.VMEM((experts * capacity, variables * levels), BF16),
            pltpu.VMEM(w_hid.shape[1:], BF16),
            pltpu.VMEM(w_out.shape[1:], BF16),
            pltpu.SemaphoreType.DMA((w_hid.shape[1] + 1,)),
        ],
        32,
    )(rows, b_in, land_vec, b_hid[0], w_in[0], far(w_hid[0]), far(w_out[0]))
    made = lax.all_to_all(made, axes, split_axis=0, concat_axis=0, tiled=True)
    out = call(
        functools.partial(finish_kernel, plan),
        [VM] * (2 + len(picks)),
        shape((columns * outs, levels), F32),
    )(made, kept, *picks)
    return out.reshape(lons, lats, outs, levels)


def solution(mesh):
    in_specs = (
        P("tile", ("lat", "emu"), None, None),
        P(),
        P("tile", ("lat", "emu")),
        P("tile", ("lat", "emu")),
        P("tile", "lat", "emu", None, None),
        P("tile", "lat", "emu"),
        P(("tile", "lat"), None, None),
        P(("tile", "lat"), None),
        P(("tile", "lat"), None),
        P(("tile", "lat"), None, None, None),
        P(("tile", "lat"), None, None),
        P(("tile", "lat"), None, None),
    )
    out_specs = P("tile", ("lat", "emu"), None, None)
    return jax.shard_map(body, mesh=mesh, in_specs=in_specs, out_specs=out_specs, check_vma=False)
```

```python
import functools
import math

import jax
import jax.numpy as jnp
from jax import lax
from jax.experimental import pallas as pl
from jax.experimental.pallas import tpu as pltpu
from jax.sharding import PartitionSpec as P

F32 = jnp.float32
BF16 = jnp.bfloat16
VM = pl.BlockSpec(memory_space=pltpu.VMEM)
SM = pl.BlockSpec(memory_space=pltpu.SMEM)
HB = pl.BlockSpec(memory_space=pltpu.HBM)


class Plan:
    def __init__(self, experts, capacity):
        self.experts = experts
        self.full = capacity // 16 * 16
        self.rest = capacity - self.full
        self.group = 8 // math.gcd(self.rest, 8) if self.rest else 1
        self.chunk = self.group * self.rest

    def rows(self, variables):
        return variables * (self.full + self.rest)

    def spot(self, number, variables):
        return (number % self.group) * (variables // self.group) + number // self.group


def iota(shape, dim):
    return lax.broadcasted_iota(jnp.int32, shape, dim)


def hot(match):
    return jnp.where(match, 1.0, 0.0).astype(BF16)


def spread(plan, place):
    small, large = plan.experts * plan.rest, plan.experts * plan.chunk
    row = iota((small, large), 0)
    if plan.rest & (plan.rest - 1) == 0:
        source = lax.shift_right_logical(row, plan.rest.bit_length() - 1)
    else:
        source = lax.div(row, plan.rest)
    return row + source * (plan.chunk - plan.rest) + place * plan.rest, iota((small, large), 1)


def route_kernel(plan, count_ref, routes_ref, land_ref, wind_ref, first_hbm, *refs):
    refs = list(refs)
    sem, column_ref, w_part = refs.pop(), refs.pop(), refs.pop()
    total = first_hbm.shape[0]
    copy = pltpu.make_async_copy(first_hbm.at[total - w_part.shape[0] :], w_part, sem)
    copy.start()
    flags_ref, wind_out = refs[:2]
    refs = refs[2:]
    experts = plan.experts
    columns = routes_ref.shape[1]
    lons, lats = land_ref.shape
    routes = routes_ref[...]
    active = iota((1, columns), 1) < count_ref[0, 0]
    owner = (iota((experts, columns), 0) == routes) & active
    owner_hot = hot(owner)
    earlier = hot(iota((columns, columns), 0) < iota((columns, columns), 1))
    before = jnp.dot(owner_hot, earlier, preferred_element_type=F32)
    rank = jnp.sum(jnp.where(owner, before, 0.0), axis=0, keepdims=True)
    diagonal = iota((columns, columns), 0) == iota((columns, columns), 1)

    def upright(row):
        return jnp.sum(jnp.where(diagonal, row, 0.0), axis=1, keepdims=True)

    rank_int = rank.astype(jnp.int32)
    if plan.full:
        target = jnp.where(active & (rank_int < plan.full), routes * plan.full + rank_int, -1)
        total = experts * plan.full
        refs.pop(0)[...] = hot(iota((total, columns), 0) == target)
        tall = upright(target.astype(F32)).astype(jnp.int32)
        refs.pop(0)[...] = hot(iota((columns, total), 1) == tall)
    if plan.rest:
        pack_ref, pick_ref = refs.pop(0), refs.pop(0)
        total = experts * plan.chunk
        held = active & (rank_int >= plan.full)
        base = routes * plan.chunk + rank_int - plan.full
        for place in range(plan.group):
            target = jnp.where(held, base + place * plan.rest, -1)
            pack_ref[:, place * columns : (place + 1) * columns] = hot(
                iota((total, columns), 0) == target
            )
            tall = upright(target.astype(F32)).astype(jnp.int32)
            pick_ref[:, place * total : (place + 1) * total] = hot(
                iota((columns, total), 1) == tall
            )
    eye = iota((lats, lats), 0) == iota((lats, lats), 1)
    for lon in range(lons):
        rows = slice(lon * lats, (lon + 1) * lats)
        flag = jnp.where(eye, land_ref[lon : lon + 1, :].astype(F32), 0.0)
        column_ref[rows, :] = jnp.broadcast_to(
            jnp.sum(flag, axis=1, keepdims=True), (lats, column_ref.shape[1])
        )
        half = jnp.where(eye, 0.5 * wind_ref[lon : lon + 1, :], 0.0)
        wind_out[rows, :] = jnp.broadcast_to(
            jnp.sum(half, axis=1, keepdims=True), (lats, wind_out.shape[1])
        )
    lanes = flags_ref.shape[1]
    at = upright(rank).astype(jnp.int32) == iota((columns, lanes), 1)
    marked = jnp.where(at, column_ref[...], 0.0).astype(BF16)
    flags_ref[...] = jnp.dot(owner_hot, marked, preferred_element_type=F32)
    copy.wait()


def band_place():
    number = lax.axis_index("lat") * lax.axis_size("emu") + lax.axis_index("emu")
    return lax.rem(number, 2) == 0


def edge_kernel(*refs):
    *refs, outer_ref, top_ref, bottom_ref, inner_ref, sems = refs
    half = len(refs) // 2
    copies = [
        pltpu.make_async_copy(source.at[: target.shape[0]], target, sems.at[k])
        for k, (source, target) in enumerate(zip(refs[:half], refs[half:]))
    ]
    for copy in copies:
        copy.start()
    copies[0].wait()
    state_ref = refs[half]
    lats = state_ref.shape[2]
    top_ref[...] = state_ref[state_ref.shape[0] - 1].astype(BF16)
    bottom_ref[...] = state_ref[0].astype(BF16)
    first, last = state_ref[:, :, 0, :], state_ref[:, :, lats - 1, :]
    even = band_place()
    inner_ref[...] = jnp.where(even, last, first).astype(BF16)
    outer_ref[...] = jnp.where(even, first, last).astype(BF16)
    for copy in copies[1:]:
        copy.wait()


def stencil_kernel(
    plan, state_ref, outer_ref, west_ref, east_ref, inner_ref, diff_ref, wind_ref, flags_ref, *refs
):
    refs = list(refs)
    even = band_place()
    pack_full = refs.pop(0) if plan.full else None
    pack_rest = refs.pop(0) if plan.rest else None
    out_ref, kept_ref, feature_ref = refs
    lons, variables, lats, levels = state_ref.shape
    columns = lons * lats
    kept = kept_ref.shape[1]
    row = iota((lats, levels), 0)
    inner_rows, outer_rows = inner_ref[...].astype(F32), outer_ref[...].astype(F32)
    for number in range(variables):
        spread_by = diff_ref[number : number + 1, :]
        spot = plan.spot(number, variables)
        for lon in range(lons):
            center = state_ref[lon, number]
            east = state_ref[lon + 1, number] if lon + 1 < lons else east_ref[number].astype(F32)
            west = state_ref[lon - 1, number] if lon else west_ref[number].astype(F32)
            inner = inner_rows[lon, number : number + 1, :]
            outer = outer_rows[lon, number : number + 1, :]
            north = jnp.where(
                row == lats - 1,
                jnp.where(even, inner, outer),
                pltpu.roll(center, lats - 1, 0),
            )
            south = jnp.where(
                row == 0, jnp.where(even, outer, inner), pltpu.roll(center, 1, 0)
            )
            total = east + west + north + south - 4.0 * center
            half = wind_ref[lon * lats : (lon + 1) * lats, :]
            moved = center + spread_by * total - half * (east - west)
            if number < kept:
                kept_ref[lon, number] = moved
            feature_ref[lon * lats : (lon + 1) * lats, spot * levels : (spot + 1) * levels] = (
                moved.astype(BF16)
            )
    experts = plan.experts
    if plan.full:
        packed = jnp.dot(pack_full[...], feature_ref[...], preferred_element_type=F32)
        for number in range(variables):
            spot = plan.spot(number, variables)
            block = packed[:, spot * levels : (spot + 1) * levels].astype(BF16)
            out_ref[:, number * plan.full : (number + 1) * plan.full, :] = block.reshape(
                experts, plan.full, levels
            )
    start = variables * plan.full
    if plan.rest:
        groups = variables // plan.group
        packed = jnp.zeros((experts * plan.chunk, groups * levels), F32)
        for place in range(plan.group):
            packed += jnp.dot(
                pack_rest[:, place * columns : (place + 1) * columns],
                feature_ref[:, place * groups * levels : (place + 1) * groups * levels],
                preferred_element_type=F32,
            )
        for group in range(groups):
            block = packed[:, group * levels : (group + 1) * levels]
            out_ref[:, start : start + plan.chunk, :] = block.reshape(
                experts, plan.chunk, levels
            ).astype(BF16)
            start += plan.chunk
    out_ref[:, start : start + 8, :] = jnp.broadcast_to(
        flags_ref[...].reshape(experts, 1, levels), (experts, 8, levels)
    ).astype(BF16)


def network_kernel(
    plan,
    rows_ref,
    b_first,
    land_add,
    b_inner,
    w_head,
    w_tail,
    w_inner,
    w_last,
    out_ref,
    x_ref,
):
    sources, _, levels = rows_ref.shape
    step = w_head.shape[0]
    variables = (step + w_tail.shape[0]) // levels
    lead = sources * plan.full
    small = sources * plan.rest
    marks = rows_ref[:, plan.rows(variables) :, :].astype(F32)
    flags = []
    if plan.full:
        for number in range(variables):
            block = rows_ref[:, number * plan.full : (number + 1) * plan.full, :]
            x_ref[:lead, number * levels : (number + 1) * levels] = block.reshape(lead, levels)
        tall = jnp.concatenate([marks] * (plan.full // 8), axis=1)
        match = iota(tall.shape, 1) == iota(tall.shape, 2)
        flags.append(jnp.sum(jnp.where(match, tall, 0.0), axis=2, keepdims=True).reshape(lead, 1))
    if plan.rest:
        start = variables * plan.full
        groups = variables // plan.group
        blocks = []
        for group in range(groups):
            block = rows_ref[:, start : start + plan.chunk, :].astype(F32)
            blocks.append(block.reshape(sources * plan.chunk, levels).astype(BF16))
            start += plan.chunk
        mixed = jnp.concatenate(blocks, axis=1)
        for place in range(plan.group):
            target, column = spread(plan, place)
            picked = jnp.dot(hot(target == column), mixed, preferred_element_type=F32)
            for group in range(groups):
                number = group * plan.group + place
                x_ref[lead:, number * levels : (number + 1) * levels] = picked[
                    :, group * levels : (group + 1) * levels
                ].astype(BF16)
        tall = jnp.concatenate([marks] * (plan.chunk // 8), axis=1)
        match = iota(tall.shape, 2) == iota(tall.shape, 1) + plan.full
        tall = jnp.sum(jnp.where(match, tall, 0.0), axis=2, keepdims=True)
        tall = jnp.broadcast_to(tall, (sources, plan.chunk, levels))
        tall = tall.reshape(sources * plan.chunk, levels).astype(BF16)
        target, column = spread(plan, 0)
        flags.append(jnp.dot(hot(target == column), tall, preferred_element_type=F32)[:, :1])
    flag = jnp.concatenate(flags, axis=0)
    pre = jnp.dot(x_ref[:, :step], w_head[...], preferred_element_type=F32) + b_first[...]
    pre += jnp.dot(x_ref[:, step:], w_tail[...], preferred_element_type=F32)
    hidden = jax.nn.silu(pre + flag * land_add[...]).astype(BF16)
    for number in range(w_inner.shape[0]):
        pre = jnp.dot(hidden, w_inner[number], preferred_element_type=F32)
        hidden = jax.nn.silu(pre + b_inner[number : number + 1, :]).astype(BF16)
    made = jnp.dot(hidden, w_last[...], preferred_element_type=F32).astype(BF16)
    outs = made.shape[1] // levels
    if plan.full:
        for number in range(outs):
            block = made[:lead, number * levels : (number + 1) * levels]
            out_ref[:, number * plan.full : (number + 1) * plan.full, :] = block.reshape(
                sources, plan.full, levels
            )
    if plan.rest:
        start = outs * plan.full
        groups = outs // plan.group
        packed = jnp.zeros((sources * plan.chunk, groups * levels), F32)
        for place in range(plan.group):
            parts = [
                made[lead:, number * levels : (number + 1) * levels]
                for number in range(place, outs, plan.group)
            ]
            part = jnp.concatenate(parts, axis=1)
            target, column = spread(plan, place)
            packed += lax.dot_general(
                hot(target == column), part, (((0,), (0,)), ((), ())), preferred_element_type=F32
            )
        for group in range(groups):
            block = packed[:, group * levels : (group + 1) * levels]
            out_ref[:, start : start + plan.chunk, :] = block.reshape(
                sources, plan.chunk, levels
            ).astype(BF16)
            start += plan.chunk


def finish_kernel(plan, rows_ref, kept_ref, *refs):
    refs = list(refs)
    pick_full = refs.pop(0) if plan.full else None
    pick_rest = refs.pop(0) if plan.rest else None
    (out_ref,) = refs
    experts, _, levels = rows_ref.shape
    lons, outs, lats, _ = kept_ref.shape
    columns = lons * lats
    found = [None] * outs
    if plan.full:
        blocks = [
            rows_ref[:, number * plan.full : (number + 1) * plan.full, :].reshape(
                experts * plan.full, levels
            )
            for number in range(outs)
        ]
        full = jnp.dot(
            pick_full[...], jnp.concatenate(blocks, axis=1), preferred_element_type=F32
        )
        found = [full[:, number * levels : (number + 1) * levels] for number in range(outs)]
    if plan.rest:
        start = outs * plan.full
        groups = outs // plan.group
        total = experts * plan.chunk
        blocks = []
        for group in range(groups):
            block = rows_ref[:, start : start + plan.chunk, :].astype(F32)
            blocks.append(block.reshape(total, levels).astype(BF16))
            start += plan.chunk
        mixed = jnp.concatenate(blocks, axis=1)
        for place in range(plan.group):
            part = jnp.dot(
                pick_rest[:, place * total : (place + 1) * total],
                mixed,
                preferred_element_type=F32,
            )
            for group in range(groups):
                number = group * plan.group + place
                piece = part[:, group * levels : (group + 1) * levels]
                found[number] = piece if found[number] is None else found[number] + piece
    for number in range(outs):
        base = kept_ref[:, number].reshape(columns, levels)
        out_ref[pl.ds(number, columns, stride=outs), :] = base + found[number]


def call(kernel, specs, shapes, scratch=(), room=12):
    return pl.pallas_call(
        kernel,
        in_specs=specs,
        out_specs=jax.tree.map(lambda _: VM, shapes),
        out_shape=shapes,
        scratch_shapes=list(scratch),
        compiler_params=pltpu.CompilerParams(vmem_limit_bytes=room * 1024 * 1024),
    )


def shape(dims, dtype):
    return jax.ShapeDtypeStruct(tuple(dims), dtype)


def far(values):
    return pltpu.with_memory_space_constraint(values, pltpu.HBM)


def exchanged(head, state, *others):
    lons, variables, lats, levels = state.shape
    lon_edge = shape((variables, lats, levels), BF16)
    lat_edge = shape((lons, variables, levels), BF16)
    values = (state,) + others
    *values, outer, top, bottom, inner = call(
        edge_kernel,
        [HB] * len(values),
        [shape(v.shape, v.dtype) for v in values[:-1]]
        + [shape((head, values[-1].shape[1]), BF16)]
        + [lat_edge, lon_edge, lon_edge, lat_edge],
        [pltpu.SemaphoreType.DMA((len(values),))],
    )(*[far(v) for v in values])
    tiles = lax.axis_size("tile")
    bands = lax.axis_size("lat") * lax.axis_size("emu")
    up = [(i, (i + 1) % tiles) for i in range(tiles)]

    def swap(values, start):
        pairs = [(i, i + 1) for i in range(start, bands - 1, 2)]
        return lax.ppermute(values, ("lat", "emu"), pairs + [(b, a) for a, b in pairs])

    outer = swap(outer, 1)
    west = lax.ppermute(top, "tile", up)
    east = lax.ppermute(bottom, "tile", [(b, a) for a, b in up])
    inner = swap(inner, 0)
    return values, (outer, west, east, inner)


def body(
    state, diffusivity, wind, land_mask, routes, counts, w_in, b_in, land_vec, w_hid, b_hid, w_out
):
    lons, lats, variables, levels = state.shape
    columns = lons * lats
    outs = w_out.shape[2] // levels
    experts = lax.axis_size("tile") * lax.axis_size("lat")
    capacity = max(2, columns * 5 // (4 * experts))
    plan = Plan(experts, capacity)
    state = jnp.transpose(state, (0, 2, 1, 3))
    w_in = far(w_in[0])
    head = w_in.shape[0] // 2
    (state, diffusivity, wind, land_mask, routes, b_in, land_vec, b_hid, w_head), halos = exchanged(
        head,
        state,
        diffusivity,
        wind,
        land_mask,
        routes.reshape(1, columns),
        b_in,
        land_vec,
        b_hid[0],
        w_in,
    )

    shapes = [shape((experts, levels), F32), shape((columns, levels), F32)]
    if plan.full:
        total = experts * plan.full
        shapes += [shape((total, columns), BF16), shape((columns, total), BF16)]
    if plan.rest:
        total = experts * plan.chunk
        shapes += [
            shape((total, plan.group * columns), BF16),
            shape((columns, plan.group * total), BF16),
        ]
    made = call(
        functools.partial(route_kernel, plan),
        [SM, VM, VM, VM, HB],
        shapes + [shape((w_in.shape[0] - head, w_in.shape[1]), BF16)],
        [pltpu.VMEM((columns, levels), F32), pltpu.SemaphoreType.DMA],
    )(counts.reshape(1, 1), routes, land_mask, wind, w_in)
    flags, half_wind, *made, w_tail = made
    packs, picks = made[::2], made[1::2]

    rows, kept = call(
        functools.partial(stencil_kernel, plan),
        [VM] * (8 + len(packs)),
        [
            shape((experts, plan.rows(variables) + 8, levels), BF16),
            shape((lons, outs, lats, levels), F32),
        ],
        [pltpu.VMEM((columns, variables * levels), BF16)],
    )(state, *halos, diffusivity, half_wind, flags, *packs)

    axes = ("tile", "lat")
    rows = lax.all_to_all(rows, axes, split_axis=0, concat_axis=0, tiled=True)
    made = call(
        functools.partial(network_kernel, plan),
        [VM] * 8,
        shape((experts, plan.rows(outs), levels), BF16),
        [
            pltpu.VMEM((experts * capacity, variables * levels), BF16),
        ],
        16,
    )(rows, b_in, land_vec, b_hid, w_head, w_tail, w_hid[0], w_out[0])
    made = lax.all_to_all(made, axes, split_axis=0, concat_axis=0, tiled=True)
    out = call(
        functools.partial(finish_kernel, plan),
        [VM] * (2 + len(picks)),
        shape((columns * outs, levels), F32),
    )(made, kept, *picks)
    return out.reshape(lons, lats, outs, levels)


def solution(mesh):
    in_specs = (
        P("tile", ("lat", "emu"), None, None),
        P(),
        P("tile", ("lat", "emu")),
        P("tile", ("lat", "emu")),
        P("tile", "lat", "emu", None, None),
        P("tile", "lat", "emu"),
        P(("tile", "lat"), None, None),
        P(("tile", "lat"), None),
        P(("tile", "lat"), None),
        P(("tile", "lat"), None, None, None),
        P(("tile", "lat"), None, None),
        P(("tile", "lat"), None, None),
    )
    out_specs = P("tile", ("lat", "emu"), None, None)
    return jax.shard_map(body, mesh=mesh, in_specs=in_specs, out_specs=out_specs, check_vma=False)
```

```python
import functools
import math

import jax
import jax.numpy as jnp
from jax import lax
from jax.experimental import pallas as pl
from jax.experimental.pallas import tpu as pltpu
from jax.sharding import PartitionSpec as P

F32 = jnp.float32
BF16 = jnp.bfloat16
VM = pl.BlockSpec(memory_space=pltpu.VMEM)
SM = pl.BlockSpec(memory_space=pltpu.SMEM)
HB = pl.BlockSpec(memory_space=pltpu.HBM)


class Plan:
    def __init__(self, experts, capacity):
        self.experts = experts
        self.full = capacity // 16 * 16
        self.rest = capacity - self.full
        self.group = 8 // math.gcd(self.rest, 8) if self.rest else 1
        self.chunk = self.group * self.rest

    def rows(self, variables):
        return variables * (self.full + self.rest)

    def spot(self, number, variables):
        return (number % self.group) * (variables // self.group) + number // self.group


def iota(shape, dim):
    return lax.broadcasted_iota(jnp.int32, shape, dim)


def hot(match):
    return jnp.where(match, 1.0, 0.0).astype(BF16)


def spread(plan, place):
    small, large = plan.experts * plan.rest, plan.experts * plan.chunk
    row = iota((small, large), 0)
    if plan.rest & (plan.rest - 1) == 0:
        source = lax.shift_right_logical(row, plan.rest.bit_length() - 1)
    else:
        source = lax.div(row, plan.rest)
    return row + source * (plan.chunk - plan.rest) + place * plan.rest, iota((small, large), 1)


def inside_stencil(state_ref, diff_ref, wind_ref, inside_ref):
    lons, variables, lats, levels = state_ref.shape
    row = iota((lats, levels), 0)
    for number in range(variables):
        spread_by = diff_ref[number : number + 1, :]
        for lon in range(lons):
            center = state_ref[lon, number]
            east = state_ref[lon + 1, number] if lon + 1 < lons else jnp.zeros_like(center)
            west = state_ref[lon - 1, number] if lon else jnp.zeros_like(center)
            north = jnp.where(row == lats - 1, 0.0, pltpu.roll(center, lats - 1, 0))
            south = jnp.where(row == 0, 0.0, pltpu.roll(center, 1, 0))
            total = east + west + north + south - 4.0 * center
            half = wind_ref[lon * lats : (lon + 1) * lats, :]
            inside_ref[lon, number] = center + spread_by * total - half * (east - west)


def route_kernel(
    plan, count_ref, routes_ref, land_ref, wind_ref, state_ref, diff_ref, first_hbm, *refs
):
    refs = list(refs)
    sem, column_ref, w_part, inside_ref = refs.pop(), refs.pop(), refs.pop(), refs.pop()
    total = first_hbm.shape[0]
    copy = pltpu.make_async_copy(first_hbm.at[total - w_part.shape[0] :], w_part, sem)
    copy.start()
    flags_ref, wind_out = refs[:2]
    refs = refs[2:]
    experts = plan.experts
    columns = routes_ref.shape[1]
    lons, lats = land_ref.shape
    routes = routes_ref[...]
    active = iota((1, columns), 1) < count_ref[0, 0]
    owner = (iota((experts, columns), 0) == routes) & active
    owner_hot = hot(owner)
    earlier = hot(iota((columns, columns), 0) < iota((columns, columns), 1))
    before = jnp.dot(owner_hot, earlier, preferred_element_type=F32)
    rank = jnp.sum(jnp.where(owner, before, 0.0), axis=0, keepdims=True)
    diagonal = iota((columns, columns), 0) == iota((columns, columns), 1)

    def upright(row):
        return jnp.sum(jnp.where(diagonal, row, 0.0), axis=1, keepdims=True)

    rank_int = rank.astype(jnp.int32)
    if plan.full:
        target = jnp.where(active & (rank_int < plan.full), routes * plan.full + rank_int, -1)
        total = experts * plan.full
        refs.pop(0)[...] = hot(iota((total, columns), 0) == target)
        tall = upright(target.astype(F32)).astype(jnp.int32)
        refs.pop(0)[...] = hot(iota((columns, total), 1) == tall)
    if plan.rest:
        pack_ref, pick_ref = refs.pop(0), refs.pop(0)
        total = experts * plan.chunk
        held = active & (rank_int >= plan.full)
        base = routes * plan.chunk + rank_int - plan.full
        for place in range(plan.group):
            target = jnp.where(held, base + place * plan.rest, -1)
            pack_ref[:, place * columns : (place + 1) * columns] = hot(
                iota((total, columns), 0) == target
            )
            tall = upright(target.astype(F32)).astype(jnp.int32)
            pick_ref[:, place * total : (place + 1) * total] = hot(
                iota((columns, total), 1) == tall
            )
    eye = iota((lats, lats), 0) == iota((lats, lats), 1)
    for lon in range(lons):
        rows = slice(lon * lats, (lon + 1) * lats)
        flag = jnp.where(eye, land_ref[lon : lon + 1, :].astype(F32), 0.0)
        column_ref[rows, :] = jnp.broadcast_to(
            jnp.sum(flag, axis=1, keepdims=True), (lats, column_ref.shape[1])
        )
        half = jnp.where(eye, 0.5 * wind_ref[lon : lon + 1, :], 0.0)
        wind_out[rows, :] = jnp.broadcast_to(
            jnp.sum(half, axis=1, keepdims=True), (lats, wind_out.shape[1])
        )
    lanes = flags_ref.shape[1]
    at = upright(rank).astype(jnp.int32) == iota((columns, lanes), 1)
    marked = jnp.where(at, column_ref[...], 0.0).astype(BF16)
    flags_ref[...] = jnp.dot(owner_hot, marked, preferred_element_type=F32)
    inside_stencil(state_ref, diff_ref, wind_out, inside_ref)
    copy.wait()


def band_place():
    number = lax.axis_index("lat") * lax.axis_size("emu") + lax.axis_index("emu")
    return lax.rem(number, 2) == 0


def edge_kernel(*refs):
    *refs, outer_ref, top_ref, bottom_ref, inner_ref, sems = refs
    half = len(refs) // 2
    copies = [
        pltpu.make_async_copy(source.at[: target.shape[0]], target, sems.at[k])
        for k, (source, target) in enumerate(zip(refs[:half], refs[half:]))
    ]
    for copy in copies:
        copy.start()
    copies[0].wait()
    state_ref = refs[half]
    lats = state_ref.shape[2]
    top_ref[...] = state_ref[state_ref.shape[0] - 1].astype(BF16)
    bottom_ref[...] = state_ref[0].astype(BF16)
    first, last = state_ref[:, :, 0, :], state_ref[:, :, lats - 1, :]
    even = band_place()
    inner_ref[...] = jnp.where(even, last, first).astype(BF16)
    outer_ref[...] = jnp.where(even, first, last).astype(BF16)
    for copy in copies[1:]:
        copy.wait()


def stencil_kernel(
    plan, inside_ref, outer_ref, west_ref, east_ref, inner_ref, diff_ref, wind_ref, flags_ref, *refs
):
    refs = list(refs)
    even = band_place()
    pack_full = refs.pop(0) if plan.full else None
    pack_rest = refs.pop(0) if plan.rest else None
    out_ref, kept_ref, feature_ref = refs
    lons, variables, lats, levels = inside_ref.shape
    columns = lons * lats
    kept = kept_ref.shape[1]
    row = iota((lats, levels), 0)
    inner, outer = inner_ref[...].astype(F32), outer_ref[...].astype(F32)
    north = jnp.where(even, inner, outer) * diff_ref[...]
    south = jnp.where(even, outer, inner) * diff_ref[...]
    for number in range(variables):
        spread_by = diff_ref[number : number + 1, :]
        spot = plan.spot(number, variables)
        for lon in range(lons):
            above = jnp.where(row == lats - 1, north[lon, number : number + 1, :], 0.0)
            below = jnp.where(row == 0, south[lon, number : number + 1, :], above)
            moved = inside_ref[lon, number] + below
            half = wind_ref[lon * lats : (lon + 1) * lats, :]
            if lon == 0:
                moved += (spread_by + half) * west_ref[number].astype(F32)
            if lon == lons - 1:
                moved += (spread_by - half) * east_ref[number].astype(F32)
            if number < kept:
                kept_ref[lon, number] = moved
            feature_ref[lon * lats : (lon + 1) * lats, spot * levels : (spot + 1) * levels] = (
                moved.astype(BF16)
            )
    experts = plan.experts
    if plan.full:
        packed = jnp.dot(pack_full[...], feature_ref[...], preferred_element_type=F32)
        for number in range(variables):
            spot = plan.spot(number, variables)
            block = packed[:, spot * levels : (spot + 1) * levels].astype(BF16)
            out_ref[:, number * plan.full : (number + 1) * plan.full, :] = block.reshape(
                experts, plan.full, levels
            )
    start = variables * plan.full
    if plan.rest:
        groups = variables // plan.group
        packed = jnp.zeros((experts * plan.chunk, groups * levels), F32)
        for place in range(plan.group):
            packed += jnp.dot(
                pack_rest[:, place * columns : (place + 1) * columns],
                feature_ref[:, place * groups * levels : (place + 1) * groups * levels],
                preferred_element_type=F32,
            )
        for group in range(groups):
            block = packed[:, group * levels : (group + 1) * levels]
            out_ref[:, start : start + plan.chunk, :] = block.reshape(
                experts, plan.chunk, levels
            ).astype(BF16)
            start += plan.chunk
    out_ref[:, start : start + 8, :] = jnp.broadcast_to(
        flags_ref[...].reshape(experts, 1, levels), (experts, 8, levels)
    ).astype(BF16)


def network_kernel(
    plan,
    rows_ref,
    b_first,
    land_add,
    b_inner,
    w_head,
    w_tail,
    w_inner,
    w_last,
    out_ref,
    x_ref,
):
    sources, _, levels = rows_ref.shape
    step = w_head.shape[0]
    variables = (step + w_tail.shape[0]) // levels
    lead = sources * plan.full
    small = sources * plan.rest
    marks = rows_ref[:, plan.rows(variables) :, :].astype(F32)
    flags = []
    if plan.full:
        for number in range(variables):
            block = rows_ref[:, number * plan.full : (number + 1) * plan.full, :]
            x_ref[:lead, number * levels : (number + 1) * levels] = block.reshape(lead, levels)
        tall = jnp.concatenate([marks] * (plan.full // 8), axis=1)
        match = iota(tall.shape, 1) == iota(tall.shape, 2)
        flags.append(jnp.sum(jnp.where(match, tall, 0.0), axis=2, keepdims=True).reshape(lead, 1))
    if plan.rest:
        start = variables * plan.full
        groups = variables // plan.group
        blocks = []
        for group in range(groups):
            block = rows_ref[:, start : start + plan.chunk, :].astype(F32)
            blocks.append(block.reshape(sources * plan.chunk, levels).astype(BF16))
            start += plan.chunk
        mixed = jnp.concatenate(blocks, axis=1)
        for place in range(plan.group):
            target, column = spread(plan, place)
            picked = jnp.dot(hot(target == column), mixed, preferred_element_type=F32)
            for group in range(groups):
                number = group * plan.group + place
                x_ref[lead:, number * levels : (number + 1) * levels] = picked[
                    :, group * levels : (group + 1) * levels
                ].astype(BF16)
        tall = jnp.concatenate([marks] * (plan.chunk // 8), axis=1)
        match = iota(tall.shape, 2) == iota(tall.shape, 1) + plan.full
        tall = jnp.sum(jnp.where(match, tall, 0.0), axis=2, keepdims=True)
        tall = jnp.broadcast_to(tall, (sources, plan.chunk, levels))
        tall = tall.reshape(sources * plan.chunk, levels).astype(BF16)
        target, column = spread(plan, 0)
        flags.append(jnp.dot(hot(target == column), tall, preferred_element_type=F32)[:, :1])
    flag = jnp.concatenate(flags, axis=0)
    pre = jnp.dot(x_ref[:, :step], w_head[...], preferred_element_type=F32) + b_first[...]
    pre += jnp.dot(x_ref[:, step:], w_tail[...], preferred_element_type=F32)
    hidden = jax.nn.silu(pre + flag * land_add[...]).astype(BF16)
    for number in range(w_inner.shape[0]):
        pre = jnp.dot(hidden, w_inner[number], preferred_element_type=F32)
        hidden = jax.nn.silu(pre + b_inner[number : number + 1, :]).astype(BF16)
    made = jnp.dot(hidden, w_last[...], preferred_element_type=F32).astype(BF16)
    outs = made.shape[1] // levels
    if plan.full:
        for number in range(outs):
            block = made[:lead, number * levels : (number + 1) * levels]
            out_ref[:, number * plan.full : (number + 1) * plan.full, :] = block.reshape(
                sources, plan.full, levels
            )
    if plan.rest:
        start = outs * plan.full
        groups = outs // plan.group
        packed = jnp.zeros((sources * plan.chunk, groups * levels), F32)
        for place in range(plan.group):
            parts = [
                made[lead:, number * levels : (number + 1) * levels]
                for number in range(place, outs, plan.group)
            ]
            part = jnp.concatenate(parts, axis=1)
            target, column = spread(plan, place)
            packed += lax.dot_general(
                hot(target == column), part, (((0,), (0,)), ((), ())), preferred_element_type=F32
            )
        for group in range(groups):
            block = packed[:, group * levels : (group + 1) * levels]
            out_ref[:, start : start + plan.chunk, :] = block.reshape(
                sources, plan.chunk, levels
            ).astype(BF16)
            start += plan.chunk


def finish_kernel(plan, rows_ref, kept_ref, *refs):
    refs = list(refs)
    pick_full = refs.pop(0) if plan.full else None
    pick_rest = refs.pop(0) if plan.rest else None
    (out_ref,) = refs
    experts, _, levels = rows_ref.shape
    lons, outs, lats, _ = kept_ref.shape
    columns = lons * lats
    found = [None] * outs
    if plan.full:
        blocks = [
            rows_ref[:, number * plan.full : (number + 1) * plan.full, :].reshape(
                experts * plan.full, levels
            )
            for number in range(outs)
        ]
        full = jnp.dot(
            pick_full[...], jnp.concatenate(blocks, axis=1), preferred_element_type=F32
        )
        found = [full[:, number * levels : (number + 1) * levels] for number in range(outs)]
    if plan.rest:
        start = outs * plan.full
        groups = outs // plan.group
        total = experts * plan.chunk
        blocks = []
        for group in range(groups):
            block = rows_ref[:, start : start + plan.chunk, :].astype(F32)
            blocks.append(block.reshape(total, levels).astype(BF16))
            start += plan.chunk
        mixed = jnp.concatenate(blocks, axis=1)
        for place in range(plan.group):
            part = jnp.dot(
                pick_rest[:, place * total : (place + 1) * total],
                mixed,
                preferred_element_type=F32,
            )
            for group in range(groups):
                number = group * plan.group + place
                piece = part[:, group * levels : (group + 1) * levels]
                found[number] = piece if found[number] is None else found[number] + piece
    for number in range(outs):
        base = kept_ref[:, number].reshape(columns, levels)
        out_ref[pl.ds(number, columns, stride=outs), :] = base + found[number]


def call(kernel, specs, shapes, scratch=(), room=12):
    return pl.pallas_call(
        kernel,
        in_specs=specs,
        out_specs=jax.tree.map(lambda _: VM, shapes),
        out_shape=shapes,
        scratch_shapes=list(scratch),
        compiler_params=pltpu.CompilerParams(vmem_limit_bytes=room * 1024 * 1024),
    )


def shape(dims, dtype):
    return jax.ShapeDtypeStruct(tuple(dims), dtype)


def far(values):
    return pltpu.with_memory_space_constraint(values, pltpu.HBM)


def exchanged(head, state, *others):
    lons, variables, lats, levels = state.shape
    lon_edge = shape((variables, lats, levels), BF16)
    lat_edge = shape((lons, variables, levels), BF16)
    values = (state,) + others
    *values, outer, top, bottom, inner = call(
        edge_kernel,
        [HB] * len(values),
        [shape(v.shape, v.dtype) for v in values[:-1]]
        + [shape((head, values[-1].shape[1]), BF16)]
        + [lat_edge, lon_edge, lon_edge, lat_edge],
        [pltpu.SemaphoreType.DMA((len(values),))],
    )(*[far(v) for v in values])
    tiles = lax.axis_size("tile")
    bands = lax.axis_size("lat") * lax.axis_size("emu")
    up = [(i, (i + 1) % tiles) for i in range(tiles)]

    def swap(values, start):
        pairs = [(i, i + 1) for i in range(start, bands - 1, 2)]
        return lax.ppermute(values, ("lat", "emu"), pairs + [(b, a) for a, b in pairs])

    outer = swap(outer, 1)
    west = lax.ppermute(top, "tile", up)
    east = lax.ppermute(bottom, "tile", [(b, a) for a, b in up])
    inner = swap(inner, 0)
    return values, (outer, west, east, inner)


def body(
    state, diffusivity, wind, land_mask, routes, counts, w_in, b_in, land_vec, w_hid, b_hid, w_out
):
    lons, lats, variables, levels = state.shape
    columns = lons * lats
    outs = w_out.shape[2] // levels
    experts = lax.axis_size("tile") * lax.axis_size("lat")
    capacity = max(2, columns * 5 // (4 * experts))
    plan = Plan(experts, capacity)
    state = jnp.transpose(state, (0, 2, 1, 3))
    w_in = far(w_in[0])
    head = w_in.shape[0] // 2
    (state, diffusivity, wind, land_mask, routes, b_in, land_vec, b_hid, w_head), halos = exchanged(
        head,
        state,
        diffusivity,
        wind,
        land_mask,
        routes.reshape(1, columns),
        b_in,
        land_vec,
        b_hid[0],
        w_in,
    )

    shapes = [shape((experts, levels), F32), shape((columns, levels), F32)]
    if plan.full:
        total = experts * plan.full
        shapes += [shape((total, columns), BF16), shape((columns, total), BF16)]
    if plan.rest:
        total = experts * plan.chunk
        shapes += [
            shape((total, plan.group * columns), BF16),
            shape((columns, plan.group * total), BF16),
        ]
    made = call(
        functools.partial(route_kernel, plan),
        [SM, VM, VM, VM, VM, VM, HB],
        shapes + [shape(state.shape, F32), shape((w_in.shape[0] - head, w_in.shape[1]), BF16)],
        [pltpu.VMEM((columns, levels), F32), pltpu.SemaphoreType.DMA],
    )(counts.reshape(1, 1), routes, land_mask, wind, state, diffusivity, w_in)
    flags, half_wind, *made, inside, w_tail = made
    packs, picks = made[::2], made[1::2]

    rows, kept = call(
        functools.partial(stencil_kernel, plan),
        [VM] * (8 + len(packs)),
        [
            shape((experts, plan.rows(variables) + 8, levels), BF16),
            shape((lons, outs, lats, levels), F32),
        ],
        [pltpu.VMEM((columns, variables * levels), BF16)],
    )(inside, *halos, diffusivity, half_wind, flags, *packs)

    axes = ("tile", "lat")
    rows = lax.all_to_all(rows, axes, split_axis=0, concat_axis=0, tiled=True)
    made = call(
        functools.partial(network_kernel, plan),
        [VM] * 8,
        shape((experts, plan.rows(outs), levels), BF16),
        [
            pltpu.VMEM((experts * capacity, variables * levels), BF16),
        ],
        16,
    )(rows, b_in, land_vec, b_hid, w_head, w_tail, w_hid[0], w_out[0])
    made = lax.all_to_all(made, axes, split_axis=0, concat_axis=0, tiled=True)
    out = call(
        functools.partial(finish_kernel, plan),
        [VM] * (2 + len(picks)),
        shape((columns * outs, levels), F32),
    )(made, kept, *picks)
    return out.reshape(lons, lats, outs, levels)


def solution(mesh):
    in_specs = (
        P("tile", ("lat", "emu"), None, None),
        P(),
        P("tile", ("lat", "emu")),
        P("tile", ("lat", "emu")),
        P("tile", "lat", "emu", None, None),
        P("tile", "lat", "emu"),
        P(("tile", "lat"), None, None),
        P(("tile", "lat"), None),
        P(("tile", "lat"), None),
        P(("tile", "lat"), None, None, None),
        P(("tile", "lat"), None, None),
        P(("tile", "lat"), None, None),
    )
    out_specs = P("tile", ("lat", "emu"), None, None)
    return jax.shard_map(body, mesh=mesh, in_specs=in_specs, out_specs=out_specs, check_vma=False)
```

```python
import functools
import math

import jax
import jax.numpy as jnp
from jax import lax
from jax.experimental import pallas as pl
from jax.experimental.pallas import tpu as pltpu
from jax.sharding import PartitionSpec as P

F32 = jnp.float32
BF16 = jnp.bfloat16
VM = pl.BlockSpec(memory_space=pltpu.VMEM)
SM = pl.BlockSpec(memory_space=pltpu.SMEM)
HB = pl.BlockSpec(memory_space=pltpu.HBM)


class Plan:
    def __init__(self, tiles, bands, capacity):
        self.experts = tiles * bands
        middle = sorted(range(tiles), key=lambda tile: abs(2 * tile - tiles + 1))
        self.order = [tile * bands + band for band in range(bands) for tile in middle]
        self.full = capacity // 16 * 16
        self.rest = capacity - self.full
        self.group = 8 // math.gcd(self.rest, 8) if self.rest else 1
        self.chunk = self.group * self.rest

    def rows(self, variables):
        return variables * (self.full + self.rest)

    def spot(self, number, variables):
        return (number % self.group) * (variables // self.group) + number // self.group


def iota(shape, dim):
    return lax.broadcasted_iota(jnp.int32, shape, dim)


def hot(match):
    return jnp.where(match, 1.0, 0.0).astype(BF16)


def spread(plan, place):
    small, large = plan.experts * plan.rest, plan.experts * plan.chunk
    row = iota((small, large), 0)
    if plan.rest & (plan.rest - 1) == 0:
        source = lax.shift_right_logical(row, plan.rest.bit_length() - 1)
    else:
        source = lax.div(row, plan.rest)
    return row + source * (plan.chunk - plan.rest) + place * plan.rest, iota((small, large), 1)


def inside_stencil(state_ref, diff_ref, wind_ref, inside_ref):
    lons, variables, lats, levels = state_ref.shape
    row = iota((lats, levels), 0)
    for number in range(variables):
        spread_by = diff_ref[number : number + 1, :]
        for lon in range(lons):
            center = state_ref[lon, number]
            east = state_ref[lon + 1, number] if lon + 1 < lons else jnp.zeros_like(center)
            west = state_ref[lon - 1, number] if lon else jnp.zeros_like(center)
            north = jnp.where(row == lats - 1, 0.0, pltpu.roll(center, lats - 1, 0))
            south = jnp.where(row == 0, 0.0, pltpu.roll(center, 1, 0))
            total = east + west + north + south - 4.0 * center
            half = wind_ref[lon * lats : (lon + 1) * lats, :]
            inside_ref[lon, number] = center + spread_by * total - half * (east - west)


def route_kernel(
    plan, count_ref, routes_ref, land_ref, wind_ref, state_ref, diff_ref, first_hbm, *refs
):
    refs = list(refs)
    sem, column_ref, w_part, inside_ref = refs.pop(), refs.pop(), refs.pop(), refs.pop()
    total = first_hbm.shape[0]
    copy = pltpu.make_async_copy(first_hbm.at[total - w_part.shape[0] :], w_part, sem)
    copy.start()
    flags_ref, wind_out = refs[:2]
    refs = refs[2:]
    experts = plan.experts
    columns = routes_ref.shape[1]
    lons, lats = land_ref.shape
    named = routes_ref[...]
    routes = jnp.zeros_like(named)
    for place, expert in enumerate(plan.order):
        routes = jnp.where(named == expert, place, routes)
    active = iota((1, columns), 1) < count_ref[0, 0]
    owner = (iota((experts, columns), 0) == routes) & active
    owner_hot = hot(owner)
    earlier = hot(iota((columns, columns), 0) < iota((columns, columns), 1))
    before = jnp.dot(owner_hot, earlier, preferred_element_type=F32)
    rank = jnp.sum(jnp.where(owner, before, 0.0), axis=0, keepdims=True)
    diagonal = iota((columns, columns), 0) == iota((columns, columns), 1)

    def upright(row):
        return jnp.sum(jnp.where(diagonal, row, 0.0), axis=1, keepdims=True)

    rank_int = rank.astype(jnp.int32)
    if plan.full:
        target = jnp.where(active & (rank_int < plan.full), routes * plan.full + rank_int, -1)
        total = experts * plan.full
        refs.pop(0)[...] = hot(iota((total, columns), 0) == target)
        tall = upright(target.astype(F32)).astype(jnp.int32)
        refs.pop(0)[...] = hot(iota((columns, total), 1) == tall)
    if plan.rest:
        pack_ref, pick_ref = refs.pop(0), refs.pop(0)
        total = experts * plan.chunk
        held = active & (rank_int >= plan.full)
        base = routes * plan.chunk + rank_int - plan.full
        for place in range(plan.group):
            target = jnp.where(held, base + place * plan.rest, -1)
            pack_ref[:, place * columns : (place + 1) * columns] = hot(
                iota((total, columns), 0) == target
            )
            tall = upright(target.astype(F32)).astype(jnp.int32)
            pick_ref[:, place * total : (place + 1) * total] = hot(
                iota((columns, total), 1) == tall
            )
    eye = iota((lats, lats), 0) == iota((lats, lats), 1)
    for lon in range(lons):
        rows = slice(lon * lats, (lon + 1) * lats)
        flag = jnp.where(eye, land_ref[lon : lon + 1, :].astype(F32), 0.0)
        column_ref[rows, :] = jnp.broadcast_to(
            jnp.sum(flag, axis=1, keepdims=True), (lats, column_ref.shape[1])
        )
        half = jnp.where(eye, 0.5 * wind_ref[lon : lon + 1, :], 0.0)
        wind_out[rows, :] = jnp.broadcast_to(
            jnp.sum(half, axis=1, keepdims=True), (lats, wind_out.shape[1])
        )
    lanes = flags_ref.shape[1]
    at = upright(rank).astype(jnp.int32) == iota((columns, lanes), 1)
    marked = jnp.where(at, column_ref[...], 0.0).astype(BF16)
    flags_ref[...] = jnp.dot(owner_hot, marked, preferred_element_type=F32)
    inside_stencil(state_ref, diff_ref, wind_out, inside_ref)
    copy.wait()


def band_place():
    number = lax.axis_index("lat") * lax.axis_size("emu") + lax.axis_index("emu")
    return lax.rem(number, 2) == 0


def edge_kernel(*refs):
    *refs, outer_ref, top_ref, bottom_ref, inner_ref, sems = refs
    half = len(refs) // 2
    copies = [
        pltpu.make_async_copy(source.at[: target.shape[0]], target, sems.at[k])
        for k, (source, target) in enumerate(zip(refs[:half], refs[half:]))
    ]
    for copy in copies:
        copy.start()
    copies[0].wait()
    state_ref = refs[half]
    lats = state_ref.shape[2]
    top_ref[...] = state_ref[state_ref.shape[0] - 1].astype(BF16)
    bottom_ref[...] = state_ref[0].astype(BF16)
    first, last = state_ref[:, :, 0, :], state_ref[:, :, lats - 1, :]
    even = band_place()
    inner_ref[...] = jnp.where(even, last, first).astype(BF16)
    outer_ref[...] = jnp.where(even, first, last).astype(BF16)
    for copy in copies[1:]:
        copy.wait()


def stencil_kernel(
    plan, inside_ref, outer_ref, west_ref, east_ref, inner_ref, diff_ref, wind_ref, flags_ref, *refs
):
    refs = list(refs)
    even = band_place()
    pack_full = refs.pop(0) if plan.full else None
    pack_rest = refs.pop(0) if plan.rest else None
    out_ref, kept_ref, feature_ref = refs
    lons, variables, lats, levels = inside_ref.shape
    columns = lons * lats
    kept = kept_ref.shape[1]
    row = iota((lats, levels), 0)
    inner, outer = inner_ref[...].astype(F32), outer_ref[...].astype(F32)
    north = jnp.where(even, inner, outer) * diff_ref[...]
    south = jnp.where(even, outer, inner) * diff_ref[...]
    for number in range(variables):
        spread_by = diff_ref[number : number + 1, :]
        spot = plan.spot(number, variables)
        for lon in range(lons):
            above = jnp.where(row == lats - 1, north[lon, number : number + 1, :], 0.0)
            below = jnp.where(row == 0, south[lon, number : number + 1, :], above)
            moved = inside_ref[lon, number] + below
            half = wind_ref[lon * lats : (lon + 1) * lats, :]
            if lon == 0:
                moved += (spread_by + half) * west_ref[number].astype(F32)
            if lon == lons - 1:
                moved += (spread_by - half) * east_ref[number].astype(F32)
            if number < kept:
                kept_ref[lon, number] = moved
            feature_ref[lon * lats : (lon + 1) * lats, spot * levels : (spot + 1) * levels] = (
                moved.astype(BF16)
            )
    experts = plan.experts
    if plan.full:
        packed = jnp.dot(pack_full[...], feature_ref[...], preferred_element_type=F32)
        for number in range(variables):
            spot = plan.spot(number, variables)
            block = packed[:, spot * levels : (spot + 1) * levels].astype(BF16)
            out_ref[:, number * plan.full : (number + 1) * plan.full, :] = block.reshape(
                experts, plan.full, levels
            )
    start = variables * plan.full
    if plan.rest:
        groups = variables // plan.group
        packed = jnp.zeros((experts * plan.chunk, groups * levels), F32)
        for place in range(plan.group):
            packed += jnp.dot(
                pack_rest[:, place * columns : (place + 1) * columns],
                feature_ref[:, place * groups * levels : (place + 1) * groups * levels],
                preferred_element_type=F32,
            )
        for group in range(groups):
            block = packed[:, group * levels : (group + 1) * levels]
            out_ref[:, start : start + plan.chunk, :] = block.reshape(
                experts, plan.chunk, levels
            ).astype(BF16)
            start += plan.chunk
    out_ref[:, start : start + 8, :] = jnp.broadcast_to(
        flags_ref[...].reshape(experts, 1, levels), (experts, 8, levels)
    ).astype(BF16)


def network_kernel(
    plan,
    rows_ref,
    b_first,
    land_add,
    b_inner,
    w_head,
    w_tail,
    w_inner,
    w_last,
    out_ref,
    x_ref,
):
    sources, _, levels = rows_ref.shape
    step = w_head.shape[0]
    variables = (step + w_tail.shape[0]) // levels
    lead = sources * plan.full
    small = sources * plan.rest
    marks = rows_ref[:, plan.rows(variables) :, :].astype(F32)
    flags = []
    if plan.full:
        for number in range(variables):
            block = rows_ref[:, number * plan.full : (number + 1) * plan.full, :]
            x_ref[:lead, number * levels : (number + 1) * levels] = block.reshape(lead, levels)
        tall = jnp.concatenate([marks] * (plan.full // 8), axis=1)
        match = iota(tall.shape, 1) == iota(tall.shape, 2)
        flags.append(jnp.sum(jnp.where(match, tall, 0.0), axis=2, keepdims=True).reshape(lead, 1))
    if plan.rest:
        start = variables * plan.full
        groups = variables // plan.group
        blocks = []
        for group in range(groups):
            block = rows_ref[:, start : start + plan.chunk, :].astype(F32)
            blocks.append(block.reshape(sources * plan.chunk, levels).astype(BF16))
            start += plan.chunk
        mixed = jnp.concatenate(blocks, axis=1)
        for place in range(plan.group):
            target, column = spread(plan, place)
            picked = jnp.dot(hot(target == column), mixed, preferred_element_type=F32)
            for group in range(groups):
                number = group * plan.group + place
                x_ref[lead:, number * levels : (number + 1) * levels] = picked[
                    :, group * levels : (group + 1) * levels
                ].astype(BF16)
        tall = jnp.concatenate([marks] * (plan.chunk // 8), axis=1)
        match = iota(tall.shape, 2) == iota(tall.shape, 1) + plan.full
        tall = jnp.sum(jnp.where(match, tall, 0.0), axis=2, keepdims=True)
        tall = jnp.broadcast_to(tall, (sources, plan.chunk, levels))
        tall = tall.reshape(sources * plan.chunk, levels).astype(BF16)
        target, column = spread(plan, 0)
        flags.append(jnp.dot(hot(target == column), tall, preferred_element_type=F32)[:, :1])
    flag = jnp.concatenate(flags, axis=0)
    pre = jnp.dot(x_ref[:, :step], w_head[...], preferred_element_type=F32) + b_first[...]
    pre += jnp.dot(x_ref[:, step:], w_tail[...], preferred_element_type=F32)
    hidden = jax.nn.silu(pre + flag * land_add[...]).astype(BF16)
    for number in range(w_inner.shape[0]):
        pre = jnp.dot(hidden, w_inner[number], preferred_element_type=F32)
        hidden = jax.nn.silu(pre + b_inner[number : number + 1, :]).astype(BF16)
    made = jnp.dot(hidden, w_last[...], preferred_element_type=F32).astype(BF16)
    outs = made.shape[1] // levels
    if plan.full:
        for number in range(outs):
            block = made[:lead, number * levels : (number + 1) * levels]
            out_ref[:, number * plan.full : (number + 1) * plan.full, :] = block.reshape(
                sources, plan.full, levels
            )
    if plan.rest:
        start = outs * plan.full
        groups = outs // plan.group
        packed = jnp.zeros((sources * plan.chunk, groups * levels), F32)
        for place in range(plan.group):
            parts = [
                made[lead:, number * levels : (number + 1) * levels]
                for number in range(place, outs, plan.group)
            ]
            part = jnp.concatenate(parts, axis=1)
            target, column = spread(plan, place)
            packed += lax.dot_general(
                hot(target == column), part, (((0,), (0,)), ((), ())), preferred_element_type=F32
            )
        for group in range(groups):
            block = packed[:, group * levels : (group + 1) * levels]
            out_ref[:, start : start + plan.chunk, :] = block.reshape(
                sources, plan.chunk, levels
            ).astype(BF16)
            start += plan.chunk


def finish_kernel(plan, rows_ref, kept_ref, *refs):
    refs = list(refs)
    pick_full = refs.pop(0) if plan.full else None
    pick_rest = refs.pop(0) if plan.rest else None
    (out_ref,) = refs
    experts, _, levels = rows_ref.shape
    lons, outs, lats, _ = kept_ref.shape
    columns = lons * lats
    found = [None] * outs
    if plan.full:
        blocks = [
            rows_ref[:, number * plan.full : (number + 1) * plan.full, :].reshape(
                experts * plan.full, levels
            )
            for number in range(outs)
        ]
        full = jnp.dot(
            pick_full[...], jnp.concatenate(blocks, axis=1), preferred_element_type=F32
        )
        found = [full[:, number * levels : (number + 1) * levels] for number in range(outs)]
    if plan.rest:
        start = outs * plan.full
        groups = outs // plan.group
        total = experts * plan.chunk
        blocks = []
        for group in range(groups):
            block = rows_ref[:, start : start + plan.chunk, :].astype(F32)
            blocks.append(block.reshape(total, levels).astype(BF16))
            start += plan.chunk
        mixed = jnp.concatenate(blocks, axis=1)
        for place in range(plan.group):
            part = jnp.dot(
                pick_rest[:, place * total : (place + 1) * total],
                mixed,
                preferred_element_type=F32,
            )
            for group in range(groups):
                number = group * plan.group + place
                piece = part[:, group * levels : (group + 1) * levels]
                found[number] = piece if found[number] is None else found[number] + piece
    for number in range(outs):
        base = kept_ref[:, number].reshape(columns, levels)
        out_ref[pl.ds(number, columns, stride=outs), :] = base + found[number]


def call(kernel, specs, shapes, scratch=(), room=12):
    return pl.pallas_call(
        kernel,
        in_specs=specs,
        out_specs=jax.tree.map(lambda _: VM, shapes),
        out_shape=shapes,
        scratch_shapes=list(scratch),
        compiler_params=pltpu.CompilerParams(vmem_limit_bytes=room * 1024 * 1024),
    )


def shape(dims, dtype):
    return jax.ShapeDtypeStruct(tuple(dims), dtype)


def far(values):
    return pltpu.with_memory_space_constraint(values, pltpu.HBM)


def exchanged(head, state, *others):
    lons, variables, lats, levels = state.shape
    lon_edge = shape((variables, lats, levels), BF16)
    lat_edge = shape((lons, variables, levels), BF16)
    values = (state,) + others
    *values, outer, top, bottom, inner = call(
        edge_kernel,
        [HB] * len(values),
        [shape(v.shape, v.dtype) for v in values[:-1]]
        + [shape((head, values[-1].shape[1]), BF16)]
        + [lat_edge, lon_edge, lon_edge, lat_edge],
        [pltpu.SemaphoreType.DMA((len(values),))],
    )(*[far(v) for v in values])
    tiles = lax.axis_size("tile")
    bands = lax.axis_size("lat") * lax.axis_size("emu")
    up = [(i, (i + 1) % tiles) for i in range(tiles)]

    def swap(values, start):
        pairs = [(i, i + 1) for i in range(start, bands - 1, 2)]
        return lax.ppermute(values, ("lat", "emu"), pairs + [(b, a) for a, b in pairs])

    outer = swap(outer, 1)
    west = lax.ppermute(top, "tile", up)
    east = lax.ppermute(bottom, "tile", [(b, a) for a, b in up])
    inner = swap(inner, 0)
    return values, (outer, west, east, inner)


def body(
    state, diffusivity, wind, land_mask, routes, counts, w_in, b_in, land_vec, w_hid, b_hid, w_out
):
    lons, lats, variables, levels = state.shape
    columns = lons * lats
    outs = w_out.shape[2] // levels
    tiles, bands = lax.axis_size("tile"), lax.axis_size("lat")
    experts = tiles * bands
    capacity = max(2, columns * 5 // (4 * experts))
    plan = Plan(tiles, bands, capacity)
    state = jnp.transpose(state, (0, 2, 1, 3))
    w_in = far(w_in[0])
    head = w_in.shape[0] // 2
    (state, diffusivity, wind, land_mask, routes, b_in, land_vec, b_hid, w_head), halos = exchanged(
        head,
        state,
        diffusivity,
        wind,
        land_mask,
        routes.reshape(1, columns),
        b_in,
        land_vec,
        b_hid[0],
        w_in,
    )

    shapes = [shape((experts, levels), F32), shape((columns, levels), F32)]
    if plan.full:
        total = experts * plan.full
        shapes += [shape((total, columns), BF16), shape((columns, total), BF16)]
    if plan.rest:
        total = experts * plan.chunk
        shapes += [
            shape((total, plan.group * columns), BF16),
            shape((columns, plan.group * total), BF16),
        ]
    made = call(
        functools.partial(route_kernel, plan),
        [SM, VM, VM, VM, VM, VM, HB],
        shapes + [shape(state.shape, F32), shape((w_in.shape[0] - head, w_in.shape[1]), BF16)],
        [pltpu.VMEM((columns, levels), F32), pltpu.SemaphoreType.DMA],
    )(counts.reshape(1, 1), routes, land_mask, wind, state, diffusivity, w_in)
    flags, half_wind, *made, inside, w_tail = made
    packs, picks = made[::2], made[1::2]

    rows, kept = call(
        functools.partial(stencil_kernel, plan),
        [VM] * (8 + len(packs)),
        [
            shape((experts, plan.rows(variables) + 8, levels), BF16),
            shape((lons, outs, lats, levels), F32),
        ],
        [pltpu.VMEM((columns, variables * levels), BF16)],
    )(inside, *halos, diffusivity, half_wind, flags, *packs)

    def exchange(values):
        return lax.all_to_all(
            values,
            ("tile", "lat"),
            split_axis=0,
            concat_axis=0,
            axis_index_groups=[plan.order],
            tiled=True,
        )

    rows = exchange(rows)
    made = call(
        functools.partial(network_kernel, plan),
        [VM] * 8,
        shape((experts, plan.rows(outs), levels), BF16),
        [
            pltpu.VMEM((experts * capacity, variables * levels), BF16),
        ],
        16,
    )(rows, b_in, land_vec, b_hid, w_head, w_tail, w_hid[0], w_out[0])
    made = exchange(made)
    out = call(
        functools.partial(finish_kernel, plan),
        [VM] * (2 + len(picks)),
        shape((columns * outs, levels), F32),
    )(made, kept, *picks)
    return out.reshape(lons, lats, outs, levels)


def solution(mesh):
    in_specs = (
        P("tile", ("lat", "emu"), None, None),
        P(),
        P("tile", ("lat", "emu")),
        P("tile", ("lat", "emu")),
        P("tile", "lat", "emu", None, None),
        P("tile", "lat", "emu"),
        P(("tile", "lat"), None, None),
        P(("tile", "lat"), None),
        P(("tile", "lat"), None),
        P(("tile", "lat"), None, None, None),
        P(("tile", "lat"), None, None),
        P(("tile", "lat"), None, None),
    )
    out_specs = P("tile", ("lat", "emu"), None, None)
    return jax.shard_map(body, mesh=mesh, in_specs=in_specs, out_specs=out_specs, check_vma=False)
```

```python
import functools
import math

import jax
import jax.numpy as jnp
from jax import lax
from jax.experimental import pallas as pl
from jax.experimental.pallas import tpu as pltpu
from jax.sharding import PartitionSpec as P


F32 = jnp.float32
BF16 = jnp.bfloat16
VM = pl.BlockSpec(memory_space=pltpu.VMEM)
SM = pl.BlockSpec(memory_space=pltpu.SMEM)
HB = pl.BlockSpec(memory_space=pltpu.HBM)


class Plan:
    def __init__(self, tiles, bands, capacity):
        self.experts = tiles * bands
        center = (tiles - 1) // 2
        middle = sorted(range(tiles), key=lambda tile: (tile % 2 == 0, abs(tile - center)))
        self.order = [tile * bands + band for band in range(bands) for tile in middle]
        self.full = capacity // 16 * 16
        self.rest = capacity - self.full
        self.group = 8 // math.gcd(self.rest, 8) if self.rest else 1
        self.chunk = self.group * self.rest

    def rows(self, variables):
        return variables * (self.full + self.rest)

    def spot(self, number, variables):
        return (number % self.group) * (variables // self.group) + number // self.group


def iota(shape, dim):
    return lax.broadcasted_iota(jnp.int32, shape, dim)


def hot(match):
    return jnp.where(match, 1.0, 0.0).astype(BF16)


def spread(plan, place):
    small, large = plan.experts * plan.rest, plan.experts * plan.chunk
    row = iota((small, large), 0)
    if plan.rest & (plan.rest - 1) == 0:
        source = lax.shift_right_logical(row, plan.rest.bit_length() - 1)
    else:
        source = lax.div(row, plan.rest)
    return row + source * (plan.chunk - plan.rest) + place * plan.rest, iota((small, large), 1)


def inside_stencil(state_ref, diff_ref, wind_ref, inside_ref):
    lons, variables, lats, levels = state_ref.shape
    row = iota((lats, levels), 0)
    for number in range(variables):
        spread_by = diff_ref[number : number + 1, :]
        for lon in range(lons):
            center = state_ref[lon, number]
            east = state_ref[lon + 1, number] if lon + 1 < lons else jnp.zeros_like(center)
            west = state_ref[lon - 1, number] if lon else jnp.zeros_like(center)
            north = jnp.where(row == lats - 1, 0.0, pltpu.roll(center, lats - 1, 0))
            south = jnp.where(row == 0, 0.0, pltpu.roll(center, 1, 0))
            total = east + west + north + south - 4.0 * center
            half = wind_ref[lon * lats : (lon + 1) * lats, :]
            inside_ref[lon, number] = center + spread_by * total - half * (east - west)


def route_kernel(
    plan, count_ref, routes_ref, land_ref, wind_ref, state_ref, diff_ref, inner_hbm, *refs
):
    refs = list(refs)
    sem, column_ref, w_part, inside_ref = refs.pop(), refs.pop(), refs.pop(), refs.pop()
    copy = pltpu.make_async_copy(inner_hbm.at[0], w_part, sem)
    copy.start()
    flags_ref, wind_out = refs[:2]
    refs = refs[2:]
    experts = plan.experts
    columns = routes_ref.shape[1]
    lons, lats = land_ref.shape
    named = routes_ref[...]
    routes = jnp.zeros_like(named)
    for place, expert in enumerate(plan.order):
        routes = jnp.where(named == expert, place, routes)
    active = iota((1, columns), 1) < count_ref[0, 0]
    owner = (iota((experts, columns), 0) == routes) & active
    owner_hot = hot(owner)
    earlier = hot(iota((columns, columns), 0) < iota((columns, columns), 1))
    before = jnp.dot(owner_hot, earlier, preferred_element_type=F32)
    rank = jnp.sum(jnp.where(owner, before, 0.0), axis=0, keepdims=True)
    diagonal = iota((columns, columns), 0) == iota((columns, columns), 1)

    def upright(row):
        return jnp.sum(jnp.where(diagonal, row, 0.0), axis=1, keepdims=True)

    rank_int = rank.astype(jnp.int32)
    if plan.full:
        target = jnp.where(active & (rank_int < plan.full), routes * plan.full + rank_int, -1)
        total = experts * plan.full
        refs.pop(0)[...] = hot(iota((total, columns), 0) == target)
        tall = upright(target.astype(F32)).astype(jnp.int32)
        refs.pop(0)[...] = hot(iota((columns, total), 1) == tall)
    if plan.rest:
        pack_ref, pick_ref = refs.pop(0), refs.pop(0)
        total = experts * plan.chunk
        held = active & (rank_int >= plan.full)
        base = routes * plan.chunk + rank_int - plan.full
        for place in range(plan.group):
            target = jnp.where(held, base + place * plan.rest, -1)
            pack_ref[:, place * columns : (place + 1) * columns] = hot(
                iota((total, columns), 0) == target
            )
            tall = upright(target.astype(F32)).astype(jnp.int32)
            pick_ref[:, place * total : (place + 1) * total] = hot(
                iota((columns, total), 1) == tall
            )
    eye = iota((lats, lats), 0) == iota((lats, lats), 1)
    for lon in range(lons):
        rows = slice(lon * lats, (lon + 1) * lats)
        flag = jnp.where(eye, land_ref[lon : lon + 1, :].astype(F32), 0.0)
        column_ref[rows, :] = jnp.broadcast_to(
            jnp.sum(flag, axis=1, keepdims=True), (lats, column_ref.shape[1])
        )
        half = jnp.where(eye, 0.5 * wind_ref[lon : lon + 1, :], 0.0)
        wind_out[rows, :] = jnp.broadcast_to(
            jnp.sum(half, axis=1, keepdims=True), (lats, wind_out.shape[1])
        )
    lanes = flags_ref.shape[1]
    at = upright(rank).astype(jnp.int32) == iota((columns, lanes), 1)
    marked = jnp.where(at, column_ref[...], 0.0).astype(BF16)
    flags_ref[...] = jnp.dot(owner_hot, marked, preferred_element_type=F32)
    inside_stencil(state_ref, diff_ref, wind_out, inside_ref)
    copy.wait()


def band_place():
    number = lax.axis_index("lat") * lax.axis_size("emu") + lax.axis_index("emu")
    return lax.rem(number, 2) == 0


def ends_kernel(*refs):
    state_ref, *refs = refs
    *refs, top_ref, bottom_ref, slabs_ref, sems = refs
    half = len(refs) // 2
    pairs = [(state_ref.at[state_ref.shape[0] - 1], slabs_ref.at[0])]
    pairs += [(state_ref.at[0], slabs_ref.at[1])]
    pairs += list(zip(refs[:half], refs[half:]))
    copies = [
        pltpu.make_async_copy(source, target, sems.at[k])
        for k, (source, target) in enumerate(pairs)
    ]
    for copy in copies:
        copy.start()
    for copy in copies:
        copy.wait()
    top_ref[...] = slabs_ref[0].astype(BF16)
    bottom_ref[...] = slabs_ref[1].astype(BF16)


def bands_kernel(state_ref, outer_ref, inner_ref):
    lats = state_ref.shape[2]
    first, last = state_ref[:, :, 0, :], state_ref[:, :, lats - 1, :]
    even = band_place()
    inner_ref[...] = jnp.where(even, last, first).astype(BF16)
    outer_ref[...] = jnp.where(even, first, last).astype(BF16)


def stencil_kernel(
    plan, inside_ref, outer_ref, west_ref, east_ref, inner_ref, diff_ref, wind_ref, flags_ref, *refs
):
    refs = list(refs)
    even = band_place()
    pack_full = refs.pop(0) if plan.full else None
    pack_rest = refs.pop(0) if plan.rest else None
    out_ref, kept_ref, feature_ref = refs
    lons, variables, lats, levels = inside_ref.shape
    columns = lons * lats
    kept = kept_ref.shape[1]
    row = iota((lats, levels), 0)
    inner, outer = inner_ref[...].astype(F32), outer_ref[...].astype(F32)
    north = jnp.where(even, inner, outer) * diff_ref[...]
    south = jnp.where(even, outer, inner) * diff_ref[...]
    for number in range(variables):
        spread_by = diff_ref[number : number + 1, :]
        spot = plan.spot(number, variables)
        for lon in range(lons):
            above = jnp.where(row == lats - 1, north[lon, number : number + 1, :], 0.0)
            below = jnp.where(row == 0, south[lon, number : number + 1, :], above)
            moved = inside_ref[lon, number] + below
            half = wind_ref[lon * lats : (lon + 1) * lats, :]
            if lon == 0:
                moved += (spread_by + half) * west_ref[number].astype(F32)
            if lon == lons - 1:
                moved += (spread_by - half) * east_ref[number].astype(F32)
            if number < kept:
                kept_ref[lon, number] = moved
            feature_ref[lon * lats : (lon + 1) * lats, spot * levels : (spot + 1) * levels] = (
                moved.astype(BF16)
            )
    experts = plan.experts
    if plan.full:
        packed = jnp.dot(pack_full[...], feature_ref[...], preferred_element_type=F32)
        for number in range(variables):
            spot = plan.spot(number, variables)
            block = packed[:, spot * levels : (spot + 1) * levels].astype(BF16)
            out_ref[:, number * plan.full : (number + 1) * plan.full, :] = block.reshape(
                experts, plan.full, levels
            )
    start = variables * plan.full
    if plan.rest:
        groups = variables // plan.group
        packed = jnp.zeros((experts * plan.chunk, groups * levels), F32)
        for place in range(plan.group):
            packed += jnp.dot(
                pack_rest[:, place * columns : (place + 1) * columns],
                feature_ref[:, place * groups * levels : (place + 1) * groups * levels],
                preferred_element_type=F32,
            )
        for group in range(groups):
            block = packed[:, group * levels : (group + 1) * levels]
            out_ref[:, start : start + plan.chunk, :] = block.reshape(
                experts, plan.chunk, levels
            ).astype(BF16)
            start += plan.chunk
    out_ref[:, start : start + 8, :] = jnp.broadcast_to(
        flags_ref[...].reshape(experts, 1, levels), (experts, 8, levels)
    ).astype(BF16)


def network_kernel(
    plan,
    rows_ref,
    b_first,
    land_add,
    b_inner,
    w_first,
    w_ahead,
    w_last,
    inner_hbm,
    out_ref,
    x_ref,
    w_inner,
    sems,
):
    sources, _, levels = rows_ref.shape
    variables = w_first.shape[0] // levels
    copies = [
        pltpu.make_async_copy(inner_hbm.at[k], w_inner.at[k - 1], sems.at[k - 1])
        for k in range(1, inner_hbm.shape[0])
    ]
    lead = sources * plan.full
    marks = rows_ref[:, plan.rows(variables) :, :].astype(F32)
    flags = []
    if plan.full:
        for number in range(variables):
            block = rows_ref[:, number * plan.full : (number + 1) * plan.full, :]
            x_ref[:lead, number * levels : (number + 1) * levels] = block.reshape(lead, levels)
        tall = jnp.concatenate([marks] * (plan.full // 8), axis=1)
        match = iota(tall.shape, 1) == iota(tall.shape, 2)
        flags.append(jnp.sum(jnp.where(match, tall, 0.0), axis=2, keepdims=True).reshape(lead, 1))
    if plan.rest:
        start = variables * plan.full
        groups = variables // plan.group
        blocks = []
        for _ in range(groups):
            block = rows_ref[:, start : start + plan.chunk, :].astype(F32)
            blocks.append(block.reshape(sources * plan.chunk, levels).astype(BF16))
            start += plan.chunk
        mixed = jnp.concatenate(blocks, axis=1)
        for place in range(plan.group):
            target, column = spread(plan, place)
            picked = jnp.dot(hot(target == column), mixed, preferred_element_type=F32)
            for group in range(groups):
                number = group * plan.group + place
                x_ref[lead:, number * levels : (number + 1) * levels] = picked[
                    :, group * levels : (group + 1) * levels
                ].astype(BF16)
        tall = jnp.concatenate([marks] * (plan.chunk // 8), axis=1)
        match = iota(tall.shape, 2) == iota(tall.shape, 1) + plan.full
        tall = jnp.sum(jnp.where(match, tall, 0.0), axis=2, keepdims=True)
        tall = jnp.broadcast_to(tall, (sources, plan.chunk, levels))
        tall = tall.reshape(sources * plan.chunk, levels).astype(BF16)
        target, column = spread(plan, 0)
        flags.append(jnp.dot(hot(target == column), tall, preferred_element_type=F32)[:, :1])
    for copy in copies:
        copy.start()
    flag = jnp.concatenate(flags, axis=0)
    pre = jnp.dot(x_ref[...], w_first[...], preferred_element_type=F32) + b_first[...]
    hidden = jax.nn.silu(pre + flag * land_add[...]).astype(BF16)
    for number in range(inner_hbm.shape[0]):
        if number:
            copies[number - 1].wait()
        weights = w_inner[number - 1] if number else w_ahead[...]
        pre = jnp.dot(hidden, weights, preferred_element_type=F32)
        hidden = jax.nn.silu(pre + b_inner[number : number + 1, :]).astype(BF16)
    made = jnp.dot(hidden, w_last[...], preferred_element_type=F32).astype(BF16)
    outs = made.shape[1] // levels
    if plan.full:
        for number in range(outs):
            block = made[:lead, number * levels : (number + 1) * levels]
            out_ref[:, number * plan.full : (number + 1) * plan.full, :] = block.reshape(
                sources, plan.full, levels
            )
    if plan.rest:
        start = outs * plan.full
        groups = outs // plan.group
        packed = jnp.zeros((sources * plan.chunk, groups * levels), F32)
        for place in range(plan.group):
            parts = [
                made[lead:, number * levels : (number + 1) * levels]
                for number in range(place, outs, plan.group)
            ]
            part = jnp.concatenate(parts, axis=1)
            target, column = spread(plan, place)
            packed += lax.dot_general(
                hot(target == column), part, (((0,), (0,)), ((), ())), preferred_element_type=F32
            )
        for group in range(groups):
            block = packed[:, group * levels : (group + 1) * levels]
            out_ref[:, start : start + plan.chunk, :] = block.reshape(
                sources, plan.chunk, levels
            ).astype(BF16)
            start += plan.chunk


def finish_kernel(plan, rows_ref, kept_ref, *refs):
    refs = list(refs)
    pick_full = refs.pop(0) if plan.full else None
    pick_rest = refs.pop(0) if plan.rest else None
    (out_ref,) = refs
    experts, _, levels = rows_ref.shape
    lons, outs, lats, _ = kept_ref.shape
    columns = lons * lats
    found = [None] * outs
    if plan.full:
        blocks = [
            rows_ref[:, number * plan.full : (number + 1) * plan.full, :].reshape(
                experts * plan.full, levels
            )
            for number in range(outs)
        ]
        full = jnp.dot(
            pick_full[...], jnp.concatenate(blocks, axis=1), preferred_element_type=F32
        )
        found = [full[:, number * levels : (number + 1) * levels] for number in range(outs)]
    if plan.rest:
        start = outs * plan.full
        groups = outs // plan.group
        total = experts * plan.chunk
        blocks = []
        for _ in range(groups):
            block = rows_ref[:, start : start + plan.chunk, :].astype(F32)
            blocks.append(block.reshape(total, levels).astype(BF16))
            start += plan.chunk
        mixed = jnp.concatenate(blocks, axis=1)
        for place in range(plan.group):
            part = jnp.dot(
                pick_rest[:, place * total : (place + 1) * total],
                mixed,
                preferred_element_type=F32,
            )
            for group in range(groups):
                number = group * plan.group + place
                piece = part[:, group * levels : (group + 1) * levels]
                found[number] = piece if found[number] is None else found[number] + piece
    for number in range(outs):
        base = kept_ref[:, number].reshape(columns, levels)
        out_ref[pl.ds(number, columns, stride=outs), :] = base + found[number]


def call(kernel, specs, shapes, scratch=(), room=12):
    return pl.pallas_call(
        kernel,
        in_specs=specs,
        out_specs=jax.tree.map(lambda _: VM, shapes),
        out_shape=shapes,
        scratch_shapes=list(scratch),
        compiler_params=pltpu.CompilerParams(vmem_limit_bytes=room * 1024 * 1024),
    )


def shape(dims, dtype):
    return jax.ShapeDtypeStruct(tuple(dims), dtype)


def far(values):
    return pltpu.with_memory_space_constraint(values, pltpu.HBM)


def exchanged(state, *others):
    lons, variables, lats, levels = state.shape
    lon_edge = shape((variables, lats, levels), BF16)
    lat_edge = shape((lons, variables, levels), BF16)
    *values, top, bottom = call(
        ends_kernel,
        [HB] * (1 + len(others)),
        [shape(v.shape, v.dtype) for v in others] + [lon_edge, lon_edge],
        [pltpu.VMEM((2,) + state.shape[1:], F32), pltpu.SemaphoreType.DMA((2 + len(others),))],
    )(*[far(v) for v in (state,) + others])
    tiles = lax.axis_size("tile")
    bands = lax.axis_size("lat") * lax.axis_size("emu")
    up = [(i, (i + 1) % tiles) for i in range(tiles)]

    def swap(values, start):
        pairs = [(i, i + 1) for i in range(start, bands - 1, 2)]
        return lax.ppermute(values, ("lat", "emu"), pairs + [(b, a) for a, b in pairs])

    west = lax.ppermute(top, "tile", up)
    east = lax.ppermute(bottom, "tile", [(b, a) for a, b in up])
    outer, inner = call(bands_kernel, [VM], [lat_edge, lat_edge])(state)
    outer = swap(outer, 1)
    inner = swap(inner, 0)
    return values, (outer, west, east, inner)


def body(
    state, diffusivity, wind, land_mask, routes, counts, w_in, b_in, land_vec, w_hid, b_hid, w_out
):
    lons, lats, variables, levels = state.shape
    columns = lons * lats
    outs = w_out.shape[2] // levels
    tiles, bands = lax.axis_size("tile"), lax.axis_size("lat")
    experts = tiles * bands
    capacity = max(2, columns * 5 // (4 * experts))
    plan = Plan(tiles, bands, capacity)
    state = jnp.transpose(state, (0, 2, 1, 3))
    (diffusivity, wind, land_mask, routes, b_in, land_vec, b_hid), halos = exchanged(
        state,
        diffusivity,
        wind,
        land_mask,
        routes.reshape(1, columns),
        b_in,
        land_vec,
        b_hid[0],
    )
    w_inner = far(w_hid[0])

    shapes = [shape((experts, levels), F32), shape((columns, levels), F32)]
    if plan.full:
        total = experts * plan.full
        shapes += [shape((total, columns), BF16), shape((columns, total), BF16)]
    if plan.rest:
        total = experts * plan.chunk
        shapes += [
            shape((total, plan.group * columns), BF16),
            shape((columns, plan.group * total), BF16),
        ]
    made = call(
        functools.partial(route_kernel, plan),
        [SM, VM, VM, VM, VM, VM, HB],
        shapes + [shape(state.shape, F32), shape(w_inner.shape[1:], BF16)],
        [pltpu.VMEM((columns, levels), F32), pltpu.SemaphoreType.DMA],
    )(counts.reshape(1, 1), routes, land_mask, wind, state, diffusivity, w_inner)
    flags, half_wind, *made, inside, w_ahead = made
    packs, picks = made[::2], made[1::2]

    rows, kept = call(
        functools.partial(stencil_kernel, plan),
        [VM] * (8 + len(packs)),
        [
            shape((experts, plan.rows(variables) + 8, levels), BF16),
            shape((lons, outs, lats, levels), F32),
        ],
        [pltpu.VMEM((columns, variables * levels), BF16)],
    )(inside, *halos, diffusivity, half_wind, flags, *packs)

    def exchange(values):
        return lax.all_to_all(
            values,
            ("tile", "lat"),
            split_axis=0,
            concat_axis=0,
            axis_index_groups=[plan.order],
            tiled=True,
        )

    rows = exchange(rows)
    made = call(
        functools.partial(network_kernel, plan),
        [VM] * 7 + [HB],
        shape((experts, plan.rows(outs), levels), BF16),
        [
            pltpu.VMEM((experts * capacity, variables * levels), BF16),
            pltpu.VMEM((max(1, w_inner.shape[0] - 1),) + w_inner.shape[1:], BF16),
            pltpu.SemaphoreType.DMA((max(1, w_inner.shape[0] - 1),)),
        ],
        16,
    )(rows, b_in, land_vec, b_hid, w_in[0], w_ahead, w_out[0], w_inner)
    made = exchange(made)
    out = call(
        functools.partial(finish_kernel, plan),
        [VM] * (2 + len(picks)),
        shape((columns * outs, levels), F32),
    )(made, kept, *picks)
    return out.reshape(lons, lats, outs, levels)


def solution(mesh):
    in_specs = (
        P("tile", ("lat", "emu"), None, None),
        P(),
        P("tile", ("lat", "emu")),
        P("tile", ("lat", "emu")),
        P("tile", "lat", "emu", None, None),
        P("tile", "lat", "emu"),
        P(("tile", "lat"), None, None),
        P(("tile", "lat"), None),
        P(("tile", "lat"), None),
        P(("tile", "lat"), None, None, None),
        P(("tile", "lat"), None, None),
        P(("tile", "lat"), None, None),
    )
    out_specs = P("tile", ("lat", "emu"), None, None)
    return jax.shard_map(body, mesh=mesh, in_specs=in_specs, out_specs=out_specs, check_vma=False)
```
